32 devices in a mesh: section: 4 (over y, core), seq: 8 (over z, x).
Axes of the slice: x: 2, y: 2, z: 4, core: 2. Of those that a mesh axis runs over, the one named last changes fastest.
Arguments:
- queries: bfloat16 [4, 1024, 2048], P('section', 'seq'), may hold values from -4 to 4
- memory_keys: bfloat16 [4, 1024, 2048], P('section', 'seq'), may hold values from -2.5 to 2.5
- memory_values: bfloat16 [4, 1024, 2048], P('section', 'seq'), may hold values from -4 to 4
- upstream: bfloat16 [4, 1024, 2048], P('section', 'seq'), may hold values from -4 to 4
- inner_rate: float32 [4, 32], P('section'), may hold values from 0.02 to 0.2
- checkpoints: float32 [4, 8, 32, 4096], P('section', 'seq'), may hold values from -0.75 to 0.75
Outputs:
- grad_queries: bfloat16 [4, 1024, 2048], P('section', 'seq')
- grad_keys: bfloat16 [4, 1024, 2048], P('section', 'seq')
- grad_values: bfloat16 [4, 1024, 2048], P('section', 'seq')
- adjoint_start: float32 [4, 8, 32, 4096], P('section', 'seq')
The draws below stay inside these ranges and needn't reach their ends.
All inputs are finite; a program needn't handle non-finite values.
Results may differ from the reference program's by a relative error of at most 0.001.
Values may be sent and summed in bfloat16 or wider, within the bound.
A program may use at most 128 MiB of HBM per device.

```python
import math
from functools import partial
import jax
import jax.numpy as jnp
from jax import lax

H = 32
DH = 64
MB = 64
TOK_DEV = 128
SECTIONS = 4
SHARDS = 8
TOKENS = 1024
HD = 2048


def shard_levels(own_key, shape, shards, low, high):
    level = 1.0
    for position, shards_of in shards:
        draws = jax.random.uniform(jax.random.fold_in(jax.random.fold_in(own_key, 6), position), (shards_of,), jnp.float32, low / len(shards), high / len(shards))
        level = level * jnp.repeat(jnp.exp(draws), shape[position] // shards_of).reshape((-1,) + (1,) * (len(shape) - 1 - position))
    return level


def centred(key, dims, deviation, limit, cuts=(), kind=jnp.bfloat16):
    loudness = shard_levels(key, dims, cuts, -0.22, 0.18) if cuts else 1.0
    values = jax.random.normal(key, dims, jnp.float32) * deviation * loudness
    return jnp.minimum(jnp.maximum(values, -limit), limit).astype(kind)


def setup_inputs(seed: int = 0) -> dict:
    key_list = jax.random.split(jax.random.key(seed), 7)
    queries = centred(key_list[0], (SECTIONS, TOKENS, HD), 1.0, 4.0, ((0, 4), (1, 8)))
    memory_keys = centred(key_list[1], (SECTIONS, TOKENS, HD), 1.0, 2.5, ((0, 4), (1, 8)))
    memory_values = centred(key_list[2], (SECTIONS, TOKENS, HD), 1.0, 4.0, ((0, 4), (1, 8)))
    upstream = centred(key_list[3], (SECTIONS, TOKENS, HD), 1.0, 4.0, ((0, 4), (1, 8)))
    inner_rate = jnp.clip(jnp.exp(math.log(0.2) - 2.3025851 * jax.random.uniform(key_list[4], (SECTIONS, H), jnp.float32) ** shard_levels(key_list[4], (SECTIONS, H), ((0, 4),), -0.2, 0.2)), 0.02, 0.2)
    checkpoints = centred(key_list[5], (SECTIONS, SHARDS, H, DH * DH), DH ** -0.5, 0.75, ((0, 4), (1, 8)), jnp.float32)
    return {"queries": queries, "memory_keys": memory_keys, "memory_values": memory_values, "upstream": upstream, "inner_rate": inner_rate, "checkpoints": checkpoints}


inner_product = partial(jnp.einsum, precision=lax.Precision.HIGHEST)


def lower_mask():
    row_index = lax.broadcasted_iota(jnp.int32, (MB, MB), 0)
    col_index = lax.broadcasted_iota(jnp.int32, (MB, MB), 1)
    return (row_index >= col_index).astype(jnp.float32)


def to_blocks(array):
    shaped = array.astype(jnp.float32).reshape(TOKENS // MB, MB, H, DH)
    return jnp.transpose(shaped, (0, 2, 1, 3))


def from_blocks(array):
    return jnp.transpose(array, (0, 2, 1, 3)).reshape(TOKENS, H * DH).astype(jnp.bfloat16)


def shard_major(array):
    per_shard = TOK_DEV // MB
    shaped = array.reshape((SHARDS, per_shard) + array.shape[1:])
    return jnp.swapaxes(shaped, 0, 1)


def block_major(array):
    return jnp.swapaxes(array, 0, 1).reshape((TOKENS // MB,) + array.shape[2:])


def one_section(operands):
    queries, memory_keys, memory_values, cotangent, inner_rate, checkpoints = operands
    per_shard = TOK_DEV // MB
    update_rate = (inner_rate / MB)[:, None, None]
    masked_scores = lower_mask()
    query_blocks = to_blocks(queries)
    key_blocks = to_blocks(memory_keys)
    value_blocks = to_blocks(memory_values)
    grad_blocks = to_blocks(cotangent)
    initial = checkpoints.reshape(SHARDS, H, DH, DH)

    def forward(weight_stack, pieces):
        current_key, current_value = pieces
        error_rows = inner_product("shmd,shde->shme", current_key, weight_stack) - current_value
        updated_weight = weight_stack - update_rate * inner_product("shmd,shme->shde", current_key, error_rows)
        return updated_weight, (weight_stack, error_rows)

    trails = lax.scan(forward, initial, (shard_major(key_blocks), shard_major(value_blocks)))[1]
    weight_trail = block_major(trails[0])
    error_trail = block_major(trails[1])

    def backward(adjoint_carry, pieces):
        current_query, current_key, current_gradient, current_weight, error_now = pieces
        attention_scores = inner_product("sxi,sbi->sxb", current_query, current_key) * masked_scores
        error_gradient = -update_rate * (inner_product("hmn,hme->hne", attention_scores, current_gradient) + inner_product("hnd,hde->hne", current_key, adjoint_carry))
        score_gradient = -update_rate * inner_product("hme,hne->hmn", current_gradient, error_now) * masked_scores
        query_gradient = inner_product("nyv,nxv->nyx", current_gradient, current_weight) + inner_product("clo,coq->clq", score_gradient, current_key)
        grad_key = (inner_product("hne,hde->hnd", error_gradient, current_weight)
                    - update_rate * inner_product("hne,hde->hnd", error_now, adjoint_carry)
                    + inner_product("fbw,fbe->fwe", score_gradient, current_query))
        previous_weight = adjoint_carry + inner_product("fwl,fwn->fln", current_query, current_gradient) + inner_product("wik,wiy->wky", current_key, error_gradient)
        return previous_weight, (query_gradient, grad_key, -error_gradient, previous_weight)

    empty = jnp.zeros((H, DH, DH), jnp.float32)
    results = lax.scan(backward, empty, (query_blocks, key_blocks, grad_blocks, weight_trail, error_trail), reverse=True)[1]
    starts = results[3].reshape(SHARDS, per_shard, H, DH, DH)[:, 0].reshape(SHARDS, H, DH * DH)
    return from_blocks(results[0]), from_blocks(results[1]), from_blocks(results[2]), starts


def reference(queries, memory_keys, memory_values, upstream, inner_rate, checkpoints):
    cotangent = jnp.roll(upstream, -1, axis=0)
    grad_queries, grad_keys, grad_values, adjoint_start = lax.map(
        one_section, (queries, memory_keys, memory_values, cotangent, inner_rate, checkpoints))
    return grad_queries, grad_keys, grad_values, adjoint_start
```

```python
from functools import partial

import jax
import jax.numpy as jnp
from jax import lax
from jax.experimental import pallas as pl
from jax.experimental.pallas import tpu as pltpu
from jax.sharding import PartitionSpec as P

MB = 64
LANES = 128
F32 = jnp.float32
BF16 = jnp.bfloat16
MESH = pl.DeviceIdType.MESH


def passed_along(block, axis, distance):
    devices = range(lax.axis_size(axis))
    route = [((i - distance) % len(devices), i) for i in devices]
    return lax.ppermute(block, axis, route)


def nn(a, b):
    return lax.dot_general(a, b, (((1,), (0,)), ((), ())), preferred_element_type=F32)


def nt(a, b):
    return lax.dot_general(a, b, (((1,), (1,)), ((), ())), preferred_element_type=F32)


def tn(a, b):
    return lax.dot_general(a, b, (((0,), (0,)), ((), ())), preferred_element_type=F32)


def split(x):
    high = x.astype(BF16)
    return high, (x - high.astype(F32)).astype(BF16)


def stacked(parts):
    return jnp.concatenate(parts, axis=0)


def tiles(x):
    return [x[:, i : i + LANES] for i in range(0, x.shape[1], LANES)]


def diagonal(x, dh):
    per = LANES // dh
    lane = lax.broadcasted_iota(jnp.int32, (x.shape[0], LANES), 1) // dh
    masks = [(lane == i).astype(F32).astype(BF16) for i in range(per)]
    pieces = tiles(x)
    zero = jnp.zeros((x.shape[0], LANES), x.dtype)
    rows = []
    for t, piece in enumerate(pieces):
        for i in range(per):
            row = [zero] * len(pieces)
            row[t] = piece * masks[i]
            rows.append(jnp.concatenate(row, axis=1))
    return stacked(rows)


def folded(a, b, dh):
    per = LANES // dh
    lane = lax.broadcasted_iota(jnp.int32, (dh, LANES), 1) // dh
    out = []
    for left, right in zip(tiles(a), tiles(b)):
        product = tn(left, right)
        value = product[:dh]
        for i in range(1, per):
            value = jnp.where(lane == i, product[i * dh : (i + 1) * dh], value)
        out.append(value)
    return jnp.concatenate(out, axis=1)


def rows_times(x, weights, multiply=nn):
    high, low = split(x)
    both = multiply(stacked([high, low]), weights)
    return both[: x.shape[0]] + both[x.shape[0] :]


def full_times(x, weights, multiply=nn):
    return rows_times(x, weights[0], multiply) + multiply(x.astype(BF16), weights[1])


def halves(x, dh):
    high, low = split(x)
    return diagonal(high, dh), diagonal(low, dh)


def exact_times(x, weights, multiply=nn):
    return multiply(x, weights[0]) + multiply(x, weights[1])


def doubled(a, b):
    return stacked([a, a]), stacked(split(b))


def lane_index(shape, dh):
    return lax.broadcasted_iota(jnp.int32, shape, 1) % dh


def local_part(q, k, v, z, c, w, dh):
    count = len(q)
    width = c.shape[1]
    row = lax.broadcasted_iota(jnp.int32, (MB, width), 0)
    upper = (lane_index((MB, width), MB) >= row).astype(F32)
    eye = lax.broadcasted_iota(jnp.int32, (dh, width), 0) == lane_index((dh, width), dh)
    weights, errors, carried, key_part, query_grads = [], [], [], [], []
    linear, source = [], []
    for t in range(count):
        whole = halves(w, dh)
        e = exact_times(k[t], whole) - v[t].astype(F32)
        weights.append(w)
        errors.append(e)
        zd = diagonal(z[t], dh)
        qd = diagonal(q[t], dh)
        scores = nt(k[t], qd) * upper
        carry = rows_times(scores, zd)
        score_grad = rows_times(e, zd, nt) * (upper * -c)
        key_part.append(rows_times(score_grad, qd))
        sg_high, sg_low = split(score_grad)
        query_grads.append(
            exact_times(z[t], whole, nt)
            + folded(stacked([sg_high, sg_low]), stacked([k[t], k[t]]), dh)
        )
        carried.append(carry)
        high, low = split(carry * -c)
        source.append(folded(stacked([q[t], k[t], k[t]]), stacked([z[t], high, low]), dh))
        gram = folded(k[t], k[t], dh)
        linear.append(jnp.where(eye, 1.0, 0.0) - c * gram)
        if t + 1 < count:
            w = w - c * folded(*doubled(k[t], e), dh)
    a, b = linear[-1], source[-1]
    for t in range(count - 2, -1, -1):
        b = full_times(linear[t], halves(b, dh)) + source[t]
        a = full_times(linear[t], halves(a, dh))
    return weights, errors, carried, key_part, query_grads, a, b


def final_part(q, k, z, c, weights, errors, carried, key_part, g, dh):
    count = len(q)
    key_grads, value_grads = [None] * count, [None] * count
    for t in range(count - 1, -1, -1):
        whole = halves(g, dh)
        minus = c * (carried[t] + exact_times(k[t], whole))
        value_grads[t] = minus
        key_grads[t] = (
            key_part[t]
            - full_times(minus, halves(weights[t], dh), nt)
            - c * full_times(errors[t], whole, nt)
        )
        high, low = split(-minus)
        g = g + folded(stacked([q[t], k[t], k[t]]), stacked([z[t], high, low]), dh)
    return key_grads, value_grads, g


def cut(ref):
    return [ref[i : i + MB, :] for i in range(0, ref.shape[0], MB)]


def put(ref, parts):
    size = ref.shape[0] // len(parts)
    for i, part in enumerate(parts):
        ref[i * size : (i + 1) * size, :] = part.astype(ref.dtype)


def local_kernel(dh, q, k, v, z, c, w, gq, trail, err, car, kp, a, b):
    weights, errors, carried, key_part, query_grads, linear, offset = local_part(
        cut(q), cut(k), cut(v), cut(z), c[...], w[...], dh
    )
    put(gq, query_grads)
    put(trail, weights)
    put(err, errors)
    put(car, carried)
    put(kp, key_part)
    a[...] = linear
    b[...] = offset


def final_kernel(dh, q, k, z, c, trail, err, car, kp, g, gk, gv, start):
    count = q.shape[0] // MB
    weights = [trail[i * dh : (i + 1) * dh, :] for i in range(count)]
    key_grads, value_grads, first = final_part(
        cut(q), cut(k), cut(z), c[...], weights, cut(err), cut(car), cut(kp), g[...], dh
    )
    put(gk, key_grads)
    put(gv, value_grads)
    start[...] = first


def relay_kernel(dh, width, a, b, end, outgoing, send_sem, recv_sem):
    shard = lax.axis_index("seq")
    section = lax.axis_index("section")
    shards = lax.axis_size("seq")
    chunks = b.shape[1] // width
    before = (section, jnp.maximum(shard - 1, 0))
    after = (section, jnp.minimum(shard + 1, shards - 1))
    not_first = shard > 0
    not_last = shard < shards - 1
    barrier = pltpu.get_barrier_semaphore()

    @pl.when(not_first)
    def _():
        pl.semaphore_signal(barrier, inc=1, device_id=before, device_id_type=MESH)

    @pl.when(not_last)
    def _():
        pl.semaphore_signal(barrier, inc=1, device_id=after, device_id_type=MESH)

    pl.semaphore_wait(barrier, not_first.astype(jnp.int32) + not_last.astype(jnp.int32))

    def copy(i):
        lanes = pl.ds(i * width, width)
        return pltpu.make_async_remote_copy(
            src_ref=outgoing.at[:, lanes],
            dst_ref=end.at[:, lanes],
            send_sem=send_sem.at[i],
            recv_sem=recv_sem.at[i],
            device_id=before,
            device_id_type=MESH,
        )

    for i in range(chunks):
        lanes = pl.ds(i * width, width)

        @pl.when(not_last)
        def _():
            copy(i).wait_recv()
            @pl.when(not_first)
            def _():
                outgoing[:, lanes] = (
                    full_times(a[:, lanes], halves(end[:, lanes], dh)) + b[:, lanes]
                )

        @pl.when(jnp.logical_not(not_last))
        def _():
            end[:, lanes] = jnp.zeros((end.shape[0], width), F32)
            outgoing[:, lanes] = b[:, lanes]

        @pl.when(not_first)
        def _():
            copy(i).start()

    @pl.when(not_first)
    def _():
        for i in range(chunks):
            copy(i).wait_send()


def per_device(queries, memory_keys, memory_values, upstream, inner_rate, checkpoints):
    heads = inner_rate.shape[1]
    features = queries.shape[2]
    dh = features // heads
    tokens = queries.shape[1]
    width = min(2 * LANES, features)
    groups = features // width
    count = tokens // MB

    q, k, v = queries[0], memory_keys[0], memory_values[0]
    z = passed_along(upstream, "section", -1)[0]
    c = jnp.repeat(inner_rate / MB, dh, axis=1)
    initial = checkpoints.reshape(heads, dh, dh).transpose(1, 0, 2).reshape(dh, features)

    def spec(rows):
        return pl.BlockSpec((rows, width), lambda i: (0, i))

    def shape(rows, kind=F32):
        return jax.ShapeDtypeStruct((rows, features), kind)

    gq, trail, err, car, kp, a, b = pl.pallas_call(
        partial(local_kernel, dh),
        grid=(groups,),
        in_specs=[spec(tokens)] * 4 + [spec(1), spec(dh)],
        out_specs=[spec(tokens), spec(count * dh), spec(tokens), spec(tokens), spec(tokens), spec(dh), spec(dh)],
        out_shape=[shape(tokens, BF16), shape(count * dh), shape(tokens), shape(tokens), shape(tokens), shape(dh), shape(dh)],
        name="local_part",
    )(q, k, v, z, c, initial)

    vmem = pl.BlockSpec(memory_space=pltpu.VMEM)
    end = pl.pallas_call(
        partial(relay_kernel, dh, width),
        in_specs=[vmem, vmem],
        out_specs=vmem,
        out_shape=shape(dh),
        scratch_shapes=[
            pltpu.VMEM((dh, features), F32),
            pltpu.SemaphoreType.DMA((groups,)),
            pltpu.SemaphoreType.DMA((groups,)),
        ],
        compiler_params=pltpu.CompilerParams(collective_id=0, has_side_effects=True),
        name="relay",
    )(a, b)

    gk, gv, start = pl.pallas_call(
        partial(final_kernel, dh),
        grid=(groups,),
        in_specs=[spec(tokens)] * 3 + [spec(1), spec(count * dh), spec(tokens), spec(tokens), spec(tokens), spec(dh)],
        out_specs=[spec(tokens), spec(tokens), spec(dh)],
        out_shape=[shape(tokens, BF16), shape(tokens, BF16), shape(dh)],
        name="final_part",
    )(q, k, z, c, trail, err, car, kp, end)
    start = start.reshape(dh, heads, dh).transpose(1, 0, 2).reshape(1, 1, heads, dh * dh)
    return gq[None], gk[None], gv[None], start


def solution(mesh):
    return jax.shard_map(
        per_device,
        mesh=mesh,
        in_specs=(
            P("section", "seq", None),
            P("section", "seq", None),
            P("section", "seq", None),
            P("section", "seq", None),
            P("section", None),
            P("section", "seq", None, None),
        ),
        out_specs=(
            P("section", "seq", None),
            P("section", "seq", None),
            P("section", "seq", None),
            P("section", "seq", None, None),
        ),
        check_vma=False,
    )
```

```python
from functools import partial

import jax
import jax.numpy as jnp
from jax import lax
from jax.experimental import pallas as pl
from jax.experimental.pallas import tpu as pltpu
from jax.sharding import PartitionSpec as P

MB = 64
LANES = 128
F32 = jnp.float32
BF16 = jnp.bfloat16
MESH = pl.DeviceIdType.MESH


def nn(a, b):
    return lax.dot_general(a, b, (((1,), (0,)), ((), ())), preferred_element_type=F32)


def nt(a, b):
    return lax.dot_general(a, b, (((1,), (1,)), ((), ())), preferred_element_type=F32)


def tn(a, b):
    return lax.dot_general(a, b, (((0,), (0,)), ((), ())), preferred_element_type=F32)


def split(x):
    high = x.astype(BF16)
    return high, (x - high.astype(F32)).astype(BF16)


def stacked(parts):
    return jnp.concatenate(parts, axis=0)


def tiles(x):
    return [x[:, i : i + LANES] for i in range(0, x.shape[1], LANES)]


def diagonal(x, dh):
    per = LANES // dh
    lane = lax.broadcasted_iota(jnp.int32, (x.shape[0], LANES), 1) // dh
    masks = [(lane == i).astype(F32).astype(BF16) for i in range(per)]
    pieces = tiles(x)
    zero = jnp.zeros((x.shape[0], LANES), x.dtype)
    rows = []
    for t, piece in enumerate(pieces):
        for i in range(per):
            row = [zero] * len(pieces)
            row[t] = piece * masks[i]
            rows.append(jnp.concatenate(row, axis=1))
    return stacked(rows)


def folded(a, b, dh):
    per = LANES // dh
    lane = lax.broadcasted_iota(jnp.int32, (dh, LANES), 1) // dh
    out = []
    for left, right in zip(tiles(a), tiles(b)):
        product = tn(left, right)
        value = product[:dh]
        for i in range(1, per):
            value = jnp.where(lane == i, product[i * dh : (i + 1) * dh], value)
        out.append(value)
    return jnp.concatenate(out, axis=1)


def rows_times(x, weights, multiply=nn):
    high, low = split(x)
    both = multiply(stacked([high, low]), weights)
    return both[: x.shape[0]] + both[x.shape[0] :]


def full_times(x, weights, multiply=nn):
    return rows_times(x, weights[0], multiply) + multiply(x.astype(BF16), weights[1])


def halves(x, dh):
    high, low = split(x)
    return diagonal(high, dh), diagonal(low, dh)


def exact_times(x, weights, multiply=nn):
    return multiply(x, weights[0]) + multiply(x, weights[1])


def doubled(a, b):
    return stacked([a, a]), stacked(split(b))


def lane_index(shape, dh):
    return lax.broadcasted_iota(jnp.int32, shape, 1) % dh


def upper_mask(width):
    row = lax.broadcasted_iota(jnp.int32, (MB, width), 0)
    return (lane_index((MB, width), MB) >= row).astype(F32)


def weight_part(k, v, c, w, dh):
    width = c.shape[1]
    row = lax.broadcasted_iota(jnp.int32, (dh, width), 0)
    eye = jnp.where(row == lane_index((dh, width), dh), 1.0, 0.0)
    weights, errors, linear = [], [], []
    for t in range(len(k)):
        e = exact_times(k[t], halves(w, dh)) - v[t].astype(F32)
        weights.append(w)
        errors.append(e)
        linear.append(eye - c * folded(k[t], k[t], dh))
        if t + 1 < len(k):
            w = w - c * folded(*doubled(k[t], e), dh)
    a = linear[-1]
    for t in range(len(k) - 2, -1, -1):
        a = full_times(linear[t], halves(a, dh))
    return weights, errors, a


def step_back(q, k, z, error_grad, dh):
    high, low = split(error_grad)
    return folded(stacked([q, k, k]), stacked([z, high, low]), dh)


def source_part(q, k, z, c, dh):
    upper = upper_mask(c.shape[1])
    carried = [
        rows_times(nt(k[t], diagonal(q[t], dh)) * upper, diagonal(z[t], dh))
        for t in range(len(k))
    ]
    b = None
    for t in range(len(k) - 1, -1, -1):
        total = carried[t] if b is None else carried[t] + exact_times(k[t], halves(b, dh))
        update = step_back(q[t], k[t], z[t], total * -c, dh)
        b = update if b is None else b + update
    return carried, b


def score_part(q, k, z, c, weights, errors, dh):
    upper = upper_mask(c.shape[1])
    query_grads, key_part = [], []
    for t in range(len(k)):
        score_grad = rows_times(errors[t], diagonal(z[t], dh), nt) * (upper * -c)
        key_part.append(rows_times(score_grad, diagonal(q[t], dh)))
        high, low = split(score_grad)
        query_grads.append(
            exact_times(z[t], halves(weights[t], dh), nt)
            + folded(stacked([high, low]), stacked([k[t], k[t]]), dh)
        )
    return query_grads, key_part


def final_part(q, k, z, c, weights, errors, carried, key_part, g, dh):
    count = len(q)
    key_grads, value_grads = [None] * count, [None] * count
    for t in range(count - 1, -1, -1):
        whole = halves(g, dh)
        minus = c * (carried[t] + exact_times(k[t], whole))
        value_grads[t] = minus
        key_grads[t] = (
            key_part[t]
            - full_times(minus, halves(weights[t], dh), nt)
            - c * full_times(errors[t], whole, nt)
        )
        high, low = split(-minus)
        g = g + folded(stacked([q[t], k[t], k[t]]), stacked([z[t], high, low]), dh)
    return key_grads, value_grads, g


def cut(ref, lanes, size=MB):
    return [ref[i : i + size, lanes] for i in range(0, ref.shape[0], size)]


def put(ref, lanes, parts):
    size = ref.shape[0] // len(parts)
    for i, part in enumerate(parts):
        ref[i * size : (i + 1) * size, lanes] = part.astype(ref.dtype)


def kernel(
    dh, width, upstream, q, k, v, c, w0,
    gq, gk, gv, start,
    z, trail, err, car, kp, a, b, other_a, other_b, pair_a, pair_b, second_a, second_b,
    entering, leaving, back, end,
    up_sems, a_send, a_recv, b_send, b_recv, g_send, g_recv, r_send, r_recv,
):
    shard, shards = lax.axis_index("seq"), lax.axis_size("seq")
    section, sections = lax.axis_index("section"), lax.axis_size("section")
    half = q.shape[1] // 2
    chunks = half // width
    side = lax.rem(shard, 2)
    partner = (section, shard + 1 - 2 * side)
    before = (section, jnp.maximum(shard - 2, 0))
    after = (section, jnp.minimum(shard + 2, shards - 1))
    below = (lax.rem(section + sections - 1, sections), shard)
    above = (lax.rem(section + 1, sections), shard)
    not_first = shard >= 2
    not_last = shard < shards - 2

    barrier = pltpu.get_barrier_semaphore()
    for peer in (below, above, partner):
        pl.semaphore_signal(barrier, inc=1, device_id=peer, device_id_type=MESH)
    for present, peer in ((not_first, before), (not_last, after)):
        @pl.when(present)
        def _():
            pl.semaphore_signal(barrier, inc=1, device_id=peer, device_id_type=MESH)
    pl.semaphore_wait(barrier, 3 + not_first.astype(jnp.int32) + not_last.astype(jnp.int32))

    def remote(source, target, send, recv, peer):
        return pltpu.make_async_remote_copy(
            src_ref=source, dst_ref=target, send_sem=send, recv_sem=recv,
            device_id=peer, device_id_type=MESH,
        )

    upward = remote(upstream, z, up_sems.at[0], up_sems.at[1], below)
    upward.start()

    def own(i):
        return pl.ds(pl.multiple_of(side * half + i * width, width), width)

    def others(i):
        return pl.ds(pl.multiple_of((1 - side) * half + i * width, width), width)

    def place(i):
        return pl.ds(pl.multiple_of(i * width, width), width)

    def send_a(i):
        return remote(a.at[:, others(i)], other_a.at[:, place(i)], a_send.at[i], a_recv.at[i], partner)

    def send_b(i):
        return remote(b.at[:, others(i)], other_b.at[:, place(i)], b_send.at[i], b_recv.at[i], partner)

    def send_g(i):
        return remote(leaving.at[:, place(i)], entering.at[:, place(i)], g_send.at[i], g_recv.at[i], before)

    def send_r(i):
        return remote(back.at[:, place(i)], end.at[:, own(i)], r_send.at[i], r_recv.at[i], partner)

    def await_r(i):
        return remote(back.at[:, place(i)], end.at[:, others(i)], r_send.at[i], r_recv.at[i], partner)

    def weights_of(lanes):
        weights, errors, linear = weight_part(
            cut(k, lanes), cut(v, lanes), c[:, lanes], w0[:, lanes], dh
        )
        put(trail, lanes, weights)
        put(err, lanes, errors)
        a[:, lanes] = linear

    def sources_of(lanes):
        carried, offset = source_part(cut(q, lanes), cut(k, lanes), cut(z, lanes), c[:, lanes], dh)
        put(car, lanes, carried)
        b[:, lanes] = offset

    def scores_of(lanes):
        query_grads, key_part = score_part(
            cut(q, lanes), cut(k, lanes), cut(z, lanes), c[:, lanes],
            cut(trail, lanes, dh), cut(err, lanes), dh,
        )
        put(gq, lanes, query_grads)
        put(kp, lanes, key_part)

    def finals_of(lanes):
        key_grads, value_grads, first = final_part(
            cut(q, lanes), cut(k, lanes), cut(z, lanes), c[:, lanes],
            cut(trail, lanes, dh), cut(err, lanes), cut(car, lanes), cut(kp, lanes), end[:, lanes], dh,
        )
        put(gk, lanes, key_grads)
        put(gv, lanes, value_grads)
        start[:, lanes] = first

    def each(body):
        def step(i, nothing):
            body(i)
            return nothing

        lax.fori_loop(0, chunks, step, jnp.int32(0))

    def first_step(i):
        weights_of(others(i))
        weights_of(own(i))
        send_a(i).start()

    def second_step(i):
        sources_of(others(i))
        send_b(i).start()
        sources_of(own(i))

    is_even = side == 0

    def pair_step(i):
        lanes, local = own(i), place(i)
        send_a(i).wait_recv()
        send_b(i).wait_recv()
        near_a, near_b = a[:, lanes], b[:, lanes]
        far_a, far_b = other_a[:, local], other_b[:, local]
        a1 = jnp.where(is_even, far_a, near_a)
        b1 = jnp.where(is_even, far_b, near_b)
        a0 = jnp.where(is_even, near_a, far_a)
        b0 = jnp.where(is_even, near_b, far_b)
        offset = full_times(a0, halves(b1, dh)) + b0
        leaving[:, local] = offset

        @pl.when(not_first & jnp.logical_not(not_last))
        def _():
            send_g(i).start()

        pair_b[:, local] = offset
        pair_a[:, local] = full_times(a0, halves(a1, dh))
        second_a[:, local] = a1
        second_b[:, local] = b1

    def relay_step(i):
        lanes, local = own(i), place(i)
        scores_of(others(i))
        scores_of(lanes)

        @pl.when(not_last)
        def _():
            send_g(i).wait_recv()
            incoming = entering[:, local]
            whole = halves(incoming, dh)
            leaving[:, local] = full_times(pair_a[:, local], whole) + pair_b[:, local]

            @pl.when(not_first)
            def _():
                send_g(i).start()

            middle = full_times(second_a[:, local], whole) + second_b[:, local]
            back[:, local] = jnp.where(is_even, incoming, middle)
            end[:, lanes] = jnp.where(is_even, middle, incoming)

        @pl.when(jnp.logical_not(not_last))
        def _():
            middle = second_b[:, local]
            nothing = jnp.zeros_like(middle)
            back[:, local] = jnp.where(is_even, nothing, middle)
            end[:, lanes] = jnp.where(is_even, middle, nothing)

        send_r(i).start()

    def last_step(i):
        finals_of(own(i))
        await_r(i).wait_recv()
        finals_of(others(i))

    def drain(i):
        send_a(i).wait_send()
        send_b(i).wait_send()
        send_r(i).wait_send()

        @pl.when(not_first)
        def _():
            send_g(i).wait_send()

    each(first_step)
    upward.wait_recv()
    each(second_step)
    each(pair_step)
    each(relay_step)
    each(last_step)
    each(drain)
    upward.wait_send()


def per_device(queries, memory_keys, memory_values, upstream, inner_rate, checkpoints):
    heads = inner_rate.shape[1]
    features = queries.shape[2]
    dh = features // heads
    tokens = queries.shape[1]
    width = 2 * LANES
    half = features // 2
    chunks = half // width
    count = tokens // MB

    c = jnp.repeat(inner_rate / MB, dh, axis=1)
    initial = checkpoints.reshape(heads, dh, dh).transpose(1, 0, 2).reshape(dh, features)
    vmem = pl.BlockSpec(memory_space=pltpu.VMEM)
    tall = jax.ShapeDtypeStruct((tokens, features), BF16)
    whole = pltpu.VMEM((dh, features), F32)
    part = pltpu.VMEM((dh, half), F32)
    rows = pltpu.VMEM((tokens, features), F32)
    gq, gk, gv, start = pl.pallas_call(
        partial(kernel, dh, width),
        in_specs=[pl.BlockSpec(memory_space=pl.ANY)] + [vmem] * 5,
        out_specs=[vmem] * 4,
        out_shape=[tall, tall, tall, jax.ShapeDtypeStruct((dh, features), F32)],
        scratch_shapes=[
            pltpu.VMEM((tokens, features), BF16),
            pltpu.VMEM((count * dh, features), F32),
            rows, rows, rows,
            whole, whole,
            part, part, part, part, part, part, part, part, part,
            whole,
            pltpu.SemaphoreType.DMA((2,)),
        ] + [pltpu.SemaphoreType.DMA((chunks,))] * 8,
        compiler_params=pltpu.CompilerParams(collective_id=0, has_side_effects=True),
        name="layer_backward",
    )(upstream[0], queries[0], memory_keys[0], memory_values[0], c, initial)
    start = start.reshape(dh, heads, dh).transpose(1, 0, 2).reshape(1, 1, heads, dh * dh)
    return gq[None], gk[None], gv[None], start


def solution(mesh):
    return jax.shard_map(
        per_device,
        mesh=mesh,
        in_specs=(
            P("section", "seq", None),
            P("section", "seq", None),
            P("section", "seq", None),
            P("section", "seq", None),
            P("section", None),
            P("section", "seq", None, None),
        ),
        out_specs=(
            P("section", "seq", None),
            P("section", "seq", None),
            P("section", "seq", None),
            P("section", "seq", None, None),
        ),
        check_vma=False,
    )
```

```python
from functools import partial

import jax
import jax.numpy as jnp
from jax import lax
from jax.experimental import pallas as pl
from jax.experimental.pallas import tpu as pltpu
from jax.sharding import PartitionSpec as P

MB = 64
LANES = 128
F32 = jnp.float32
BF16 = jnp.bfloat16
MESH = pl.DeviceIdType.MESH


def nn(a, b):
    return lax.dot_general(a, b, (((1,), (0,)), ((), ())), preferred_element_type=F32)


def nt(a, b):
    return lax.dot_general(a, b, (((1,), (1,)), ((), ())), preferred_element_type=F32)


def tn(a, b):
    return lax.dot_general(a, b, (((0,), (0,)), ((), ())), preferred_element_type=F32)


def split(x):
    high = x.astype(BF16)
    return high, (x - high.astype(F32)).astype(BF16)


def stacked(parts):
    return jnp.concatenate(parts, axis=0)


def tiles(x):
    return [x[:, i : i + LANES] for i in range(0, x.shape[1], LANES)]


def diagonal(x, dh):
    per = LANES // dh
    lane = lax.broadcasted_iota(jnp.int32, (x.shape[0], LANES), 1) // dh
    masks = [(lane == i).astype(F32).astype(BF16) for i in range(per)]
    pieces = tiles(x)
    zero = jnp.zeros((x.shape[0], LANES), x.dtype)
    rows = []
    for t, piece in enumerate(pieces):
        for i in range(per):
            row = [zero] * len(pieces)
            row[t] = piece * masks[i]
            rows.append(jnp.concatenate(row, axis=1))
    return stacked(rows)


def folded(a, b, dh):
    per = LANES // dh
    lane = lax.broadcasted_iota(jnp.int32, (dh, LANES), 1) // dh
    out = []
    for left, right in zip(tiles(a), tiles(b)):
        product = tn(left, right)
        value = product[:dh]
        for i in range(1, per):
            value = jnp.where(lane == i, product[i * dh : (i + 1) * dh], value)
        out.append(value)
    return jnp.concatenate(out, axis=1)


def rows_times(x, weights, multiply=nn):
    high, low = split(x)
    both = multiply(stacked([high, low]), weights)
    return both[: x.shape[0]] + both[x.shape[0] :]


def full_times(x, weights, multiply=nn):
    return rows_times(x, weights[0], multiply) + multiply(x.astype(BF16), weights[1])


def halves(x, dh):
    high, low = split(x)
    return diagonal(high, dh), diagonal(low, dh)


def exact_times(x, weights, multiply=nn):
    return multiply(x, weights[0]) + multiply(x, weights[1])


def doubled(a, b):
    return stacked([a, a]), stacked(split(b))


def lane_index(shape, dh):
    return lax.broadcasted_iota(jnp.int32, shape, 1) % dh


def upper_mask(width):
    row = lax.broadcasted_iota(jnp.int32, (MB, width), 0)
    return (lane_index((MB, width), MB) >= row).astype(F32)


def weight_part(k, v, c, w, dh):
    width = c.shape[1]
    row = lax.broadcasted_iota(jnp.int32, (dh, width), 0)
    eye = jnp.where(row == lane_index((dh, width), dh), 1.0, 0.0)
    weights, errors, linear = [], [], []
    for t in range(len(k)):
        e = exact_times(k[t], halves(w, dh)) - v[t].astype(F32)
        yield
        weights.append(w)
        errors.append(e)
        if t + 1 < len(k):
            w = w - c * folded(*doubled(k[t], e), dh)
            yield
        linear.append(eye - c * folded(k[t], k[t], dh))
        yield
    a = linear[-1]
    for t in range(len(k) - 2, -1, -1):
        a = full_times(linear[t], halves(a, dh))
    return weights, errors, a


def interleaved(runs):
    results, waiting = [None] * len(runs), dict(enumerate(runs))
    while waiting:
        for i, run in list(waiting.items()):
            try:
                next(run)
            except StopIteration as stop:
                results[i] = stop.value
                del waiting[i]
    return results


def step_back(q, k, z, error_grad, dh):
    high, low = split(error_grad)
    return folded(stacked([q, k, k]), stacked([z, high, low]), dh)


def source_part(q, k, z, c, dh):
    upper = upper_mask(c.shape[1])
    carried = [None] * len(k)
    for t in range(len(k) - 1, -1, -1):
        scores = nt(k[t], diagonal(q[t], dh)) * upper
        yield
        carried[t] = rows_times(scores, diagonal(z[t], dh))
        yield
    b = None
    for t in range(len(k) - 1, -1, -1):
        total = carried[t] if b is None else carried[t] + exact_times(k[t], halves(b, dh))
        yield
        update = step_back(q[t], k[t], z[t], total * -c, dh)
        b = update if b is None else b + update
        yield
    return carried, b


def score_part(q, k, z, c, weights, errors, dh):
    upper = upper_mask(c.shape[1])
    query_grads, key_part = [], []
    for t in range(len(k)):
        score_grad = rows_times(errors[t], diagonal(z[t], dh), nt) * (upper * -c)
        yield
        key_part.append(rows_times(score_grad, diagonal(q[t], dh)))
        yield
        high, low = split(score_grad)
        query_grads.append(
            exact_times(z[t], halves(weights[t], dh), nt)
            + folded(stacked([high, low]), stacked([k[t], k[t]]), dh)
        )
        yield
    return query_grads, key_part


def final_part(q, k, z, c, weights, errors, carried, key_part, g, dh):
    count = len(q)
    key_grads, value_grads = [None] * count, [None] * count
    for t in range(count - 1, -1, -1):
        whole = halves(g, dh)
        minus = c * (carried[t] + exact_times(k[t], whole))
        yield
        value_grads[t] = minus
        g = g + step_back(q[t], k[t], z[t], -minus, dh)
        yield
        partial_grad = key_part[t] - c * full_times(errors[t], whole, nt)
        yield
        key_grads[t] = partial_grad - full_times(minus, halves(weights[t], dh), nt)
        yield
    return key_grads, value_grads, g


def cut(ref, lanes, size=MB):
    return [ref[i : i + size, lanes] for i in range(0, ref.shape[0], size)]


def put(ref, lanes, parts):
    size = ref.shape[0] // len(parts)
    for i, part in enumerate(parts):
        ref[i * size : (i + 1) * size, lanes] = part.astype(ref.dtype)


def kernel(
    dh, width, upstream, q, k, v, c, w0,
    gq, gk, gv, start,
    z, trail, err, car, kp, a, b, other_a, other_b, pair_a, pair_b, second_a, second_b,
    entering, leaving, back, end,
    up_sems, a_send, a_recv, b_send, b_recv, g_send, g_recv, r_send, r_recv,
):
    shard, shards = lax.axis_index("seq"), lax.axis_size("seq")
    section, sections = lax.axis_index("section"), lax.axis_size("section")
    half = q.shape[1] // 2
    chunks = half // width
    side = lax.rem(shard, 2)
    partner = (section, shard + 1 - 2 * side)
    before = (section, jnp.maximum(shard - 2, 0))
    after = (section, jnp.minimum(shard + 2, shards - 1))
    below = (lax.rem(section + sections - 1, sections), shard)
    above = (lax.rem(section + 1, sections), shard)
    not_first = shard >= 2
    not_last = shard < shards - 2

    barrier = pltpu.get_barrier_semaphore()
    for peer in (below, above, partner):
        pl.semaphore_signal(barrier, inc=1, device_id=peer, device_id_type=MESH)
    for present, peer in ((not_first, before), (not_last, after)):
        @pl.when(present)
        def _():
            pl.semaphore_signal(barrier, inc=1, device_id=peer, device_id_type=MESH)
    pl.semaphore_wait(barrier, 3 + not_first.astype(jnp.int32) + not_last.astype(jnp.int32))

    def remote(source, target, send, recv, peer):
        return pltpu.make_async_remote_copy(
            src_ref=source, dst_ref=target, send_sem=send, recv_sem=recv,
            device_id=peer, device_id_type=MESH,
        )

    upward = remote(upstream, z, up_sems.at[0], up_sems.at[1], below)
    upward.start()

    def own(i):
        return pl.ds(pl.multiple_of(side * half + i * width, width), width)

    def others(i):
        return pl.ds(pl.multiple_of((1 - side) * half + i * width, width), width)

    def place(i):
        return pl.ds(pl.multiple_of(i * width, width), width)

    def send_a(i):
        return remote(a.at[:, others(i)], other_a.at[:, place(i)], a_send.at[i], a_recv.at[i], partner)

    def send_b(i):
        return remote(b.at[:, others(i)], other_b.at[:, place(i)], b_send.at[i], b_recv.at[i], partner)

    def send_g(i):
        return remote(leaving.at[:, place(i)], entering.at[:, place(i)], g_send.at[i], g_recv.at[i], before)

    def send_r(i):
        return remote(back.at[:, place(i)], end.at[:, own(i)], r_send.at[i], r_recv.at[i], partner)

    def await_r(i):
        return remote(back.at[:, place(i)], end.at[:, others(i)], r_send.at[i], r_recv.at[i], partner)

    def narrow(span):
        start_lane = span.start
        return [
            pl.ds(pl.multiple_of(start_lane + j, LANES), LANES) for j in range(0, width, LANES)
        ]

    def together(compute, store, spans):
        groups = [lanes for span in spans for lanes in narrow(span)]
        results = interleaved([compute(lanes) for lanes in groups])
        for lanes, result in zip(groups, results):
            store(lanes, *result)

    def weights_of(lanes):
        return weight_part(cut(k, lanes), cut(v, lanes), c[:, lanes], w0[:, lanes], dh)

    def put_weights(lanes, weights, errors, linear):
        put(trail, lanes, weights)
        put(err, lanes, errors)
        a[:, lanes] = linear

    def sources_of(lanes):
        return source_part(cut(q, lanes), cut(k, lanes), cut(z, lanes), c[:, lanes], dh)

    def put_sources(lanes, carried, offset):
        put(car, lanes, carried)
        b[:, lanes] = offset

    def scores_of(lanes):
        return score_part(
            cut(q, lanes), cut(k, lanes), cut(z, lanes), c[:, lanes],
            cut(trail, lanes, dh), cut(err, lanes), dh,
        )

    def put_scores(lanes, query_grads, key_part):
        put(gq, lanes, query_grads)
        put(kp, lanes, key_part)

    def finals_of(lanes):
        return final_part(
            cut(q, lanes), cut(k, lanes), cut(z, lanes), c[:, lanes],
            cut(trail, lanes, dh), cut(err, lanes), cut(car, lanes), cut(kp, lanes), end[:, lanes], dh,
        )

    def put_finals(lanes, key_grads, value_grads, first):
        put(gk, lanes, key_grads)
        put(gv, lanes, value_grads)
        start[:, lanes] = first

    def each(body):
        def step(i, nothing):
            body(i)
            return nothing

        lax.fori_loop(0, chunks, step, jnp.int32(0))

    def first_step(i):
        together(weights_of, put_weights, [others(i), own(i)])
        send_a(i).start()

    def second_step(i):
        together(sources_of, put_sources, [others(i), own(i)])
        send_b(i).start()

    is_even = side == 0

    def pair_step(i):
        lanes, local = own(i), place(i)
        send_a(i).wait_recv()
        send_b(i).wait_recv()
        near_a, near_b = a[:, lanes], b[:, lanes]
        far_a, far_b = other_a[:, local], other_b[:, local]
        a1 = jnp.where(is_even, far_a, near_a)
        b1 = jnp.where(is_even, far_b, near_b)
        a0 = jnp.where(is_even, near_a, far_a)
        b0 = jnp.where(is_even, near_b, far_b)
        offset = full_times(a0, halves(b1, dh)) + b0
        leaving[:, local] = offset

        @pl.when(not_first & jnp.logical_not(not_last))
        def _():
            send_g(i).start()

        pair_b[:, local] = offset
        pair_a[:, local] = full_times(a0, halves(a1, dh))
        second_a[:, local] = a1
        second_b[:, local] = b1

    def relay_step(i):
        lanes, local = own(i), place(i)
        together(scores_of, put_scores, [others(i), lanes])

        @pl.when(not_last)
        def _():
            send_g(i).wait_recv()
            incoming = entering[:, local]
            whole = halves(incoming, dh)
            leaving[:, local] = full_times(pair_a[:, local], whole) + pair_b[:, local]

            @pl.when(not_first)
            def _():
                send_g(i).start()

            middle = full_times(second_a[:, local], whole) + second_b[:, local]
            back[:, local] = jnp.where(is_even, incoming, middle)
            end[:, lanes] = jnp.where(is_even, middle, incoming)

        @pl.when(jnp.logical_not(not_last))
        def _():
            middle = second_b[:, local]
            nothing = jnp.zeros_like(middle)
            back[:, local] = jnp.where(is_even, nothing, middle)
            end[:, lanes] = jnp.where(is_even, middle, nothing)

        send_r(i).start()

    def last_step(i):
        await_r(i).wait_recv()
        together(finals_of, put_finals, [own(i), others(i)])

    def drain(i):
        send_a(i).wait_send()
        send_b(i).wait_send()
        send_r(i).wait_send()

        @pl.when(not_first)
        def _():
            send_g(i).wait_send()

    each(first_step)
    upward.wait_recv()
    each(second_step)
    each(pair_step)
    each(relay_step)
    each(last_step)
    each(drain)
    upward.wait_send()


def per_device(queries, memory_keys, memory_values, upstream, inner_rate, checkpoints):
    heads = inner_rate.shape[1]
    features = queries.shape[2]
    dh = features // heads
    tokens = queries.shape[1]
    width = 2 * LANES
    half = features // 2
    chunks = half // width
    count = tokens // MB

    c = jnp.repeat(inner_rate / MB, dh, axis=1)
    initial = checkpoints.reshape(heads, dh, dh).transpose(1, 0, 2).reshape(dh, features)
    vmem = pl.BlockSpec(memory_space=pltpu.VMEM)
    tall = jax.ShapeDtypeStruct((tokens, features), BF16)
    whole = pltpu.VMEM((dh, features), F32)
    part = pltpu.VMEM((dh, half), F32)
    rows = pltpu.VMEM((tokens, features), F32)
    gq, gk, gv, start = pl.pallas_call(
        partial(kernel, dh, width),
        in_specs=[pl.BlockSpec(memory_space=pl.ANY)] + [vmem] * 5,
        out_specs=[vmem] * 4,
        out_shape=[tall, tall, tall, jax.ShapeDtypeStruct((dh, features), F32)],
        scratch_shapes=[
            pltpu.VMEM((tokens, features), BF16),
            pltpu.VMEM((count * dh, features), F32),
            rows, rows, rows,
            whole, whole,
            part, part, part, part, part, part, part, part, part,
            whole,
            pltpu.SemaphoreType.DMA((2,)),
        ] + [pltpu.SemaphoreType.DMA((chunks,))] * 8,
        compiler_params=pltpu.CompilerParams(collective_id=0, has_side_effects=True),
        name="layer_backward",
    )(upstream[0], queries[0], memory_keys[0], memory_values[0], c, initial)
    start = start.reshape(dh, heads, dh).transpose(1, 0, 2).reshape(1, 1, heads, dh * dh)
    return gq[None], gk[None], gv[None], start


def solution(mesh):
    return jax.shard_map(
        per_device,
        mesh=mesh,
        in_specs=(
            P("section", "seq", None),
            P("section", "seq", None),
            P("section", "seq", None),
            P("section", "seq", None),
            P("section", None),
            P("section", "seq", None, None),
        ),
        out_specs=(
            P("section", "seq", None),
            P("section", "seq", None),
            P("section", "seq", None),
            P("section", "seq", None, None),
        ),
        check_vma=False,
    )
```

```python
from functools import partial

import jax
import jax.numpy as jnp
from jax import lax
from jax.experimental import pallas as pl
from jax.experimental.pallas import tpu as pltpu
from jax.sharding import PartitionSpec as P

MB = 64
LANES = 128
F32 = jnp.float32
BF16 = jnp.bfloat16
MESH = pl.DeviceIdType.MESH


def nn(a, b):
    return lax.dot_general(a, b, (((1,), (0,)), ((), ())), preferred_element_type=F32)


def nt(a, b):
    return lax.dot_general(a, b, (((1,), (1,)), ((), ())), preferred_element_type=F32)


def tn(a, b):
    return lax.dot_general(a, b, (((0,), (0,)), ((), ())), preferred_element_type=F32)


def split(x):
    high = x.astype(BF16)
    return high, (x - high.astype(F32)).astype(BF16)


def stacked(parts):
    return jnp.concatenate(parts, axis=0)


def tiles(x):
    return [x[:, i : i + LANES] for i in range(0, x.shape[1], LANES)]


def diagonal(x, dh):
    per = LANES // dh
    lane = lax.broadcasted_iota(jnp.int32, (x.shape[0], LANES), 1) // dh
    masks = [(lane == i).astype(F32).astype(BF16) for i in range(per)]
    pieces = tiles(x)
    zero = jnp.zeros((x.shape[0], LANES), x.dtype)
    rows = []
    for t, piece in enumerate(pieces):
        for i in range(per):
            row = [zero] * len(pieces)
            row[t] = piece * masks[i]
            rows.append(jnp.concatenate(row, axis=1))
    return stacked(rows)


def folded(a, b, dh):
    per = LANES // dh
    lane = lax.broadcasted_iota(jnp.int32, (dh, LANES), 1) // dh
    out = []
    for left, right in zip(tiles(a), tiles(b)):
        product = tn(left, right)
        value = product[:dh]
        for i in range(1, per):
            value = jnp.where(lane == i, product[i * dh : (i + 1) * dh], value)
        out.append(value)
    return jnp.concatenate(out, axis=1)


def rows_times(x, weights, multiply=nn):
    high, low = split(x)
    both = multiply(stacked([high, low]), weights)
    return both[: x.shape[0]] + both[x.shape[0] :]


def full_times(x, weights, multiply=nn):
    return rows_times(x, weights[0], multiply) + multiply(x.astype(BF16), weights[1])


def halves(x, dh):
    high, low = split(x)
    return diagonal(high, dh), diagonal(low, dh)


def exact_times(x, weights, multiply=nn):
    return multiply(x, weights[0]) + multiply(x, weights[1])


def doubled(a, b):
    return stacked([a, a]), stacked(split(b))


def lane_index(shape, dh):
    return lax.broadcasted_iota(jnp.int32, shape, 1) % dh


def upper_mask(width):
    row = lax.broadcasted_iota(jnp.int32, (MB, width), 0)
    return (lane_index((MB, width), MB) >= row).astype(F32)


def weight_part(k, v, c, w, dh):
    width = c.shape[1]
    row = lax.broadcasted_iota(jnp.int32, (dh, width), 0)
    eye = jnp.where(row == lane_index((dh, width), dh), 1.0, 0.0)
    weights, errors, linear = [], [], []
    for t in range(len(k)):
        e = exact_times(k[t], halves(w, dh)) - v[t].astype(F32)
        yield
        weights.append(w)
        errors.append(e)
        if t + 1 < len(k):
            w = w - c * folded(*doubled(k[t], e), dh)
            yield
        linear.append(eye - c * folded(k[t], k[t], dh))
        yield
    a = linear[-1]
    for t in range(len(k) - 2, -1, -1):
        a = full_times(linear[t], halves(a, dh))
    return weights, errors, a


def interleaved(runs):
    results, waiting = [None] * len(runs), dict(enumerate(runs))
    while waiting:
        for i, run in list(waiting.items()):
            try:
                next(run)
            except StopIteration as stop:
                results[i] = stop.value
                del waiting[i]
    return results


def step_back(q, k, z, error_grad, dh):
    high, low = split(error_grad)
    return folded(stacked([q, k, k]), stacked([z, high, low]), dh)


def source_part(q, k, z, c, dh):
    upper = upper_mask(c.shape[1])
    carried = [None] * len(k)
    for t in range(len(k) - 1, -1, -1):
        scores = nt(k[t], diagonal(q[t], dh)) * upper
        yield
        carried[t] = rows_times(scores, diagonal(z[t], dh))
        yield
    b = None
    for t in range(len(k) - 1, -1, -1):
        total = carried[t] if b is None else carried[t] + exact_times(k[t], halves(b, dh))
        yield
        update = step_back(q[t], k[t], z[t], total * -c, dh)
        b = update if b is None else b + update
        yield
    return carried, b


def score_part(q, k, z, c, weights, errors, dh):
    upper = upper_mask(c.shape[1])
    query_grads, key_part = [], []
    for t in range(len(k)):
        score_grad = rows_times(errors[t], diagonal(z[t], dh), nt) * (upper * -c)
        yield
        key_part.append(rows_times(score_grad, diagonal(q[t], dh)))
        yield
        high, low = split(score_grad)
        query_grads.append(
            exact_times(z[t], halves(weights[t], dh), nt)
            + folded(stacked([high, low]), stacked([k[t], k[t]]), dh)
        )
        yield
    return query_grads, key_part


def final_part(q, k, z, c, weights, errors, carried, key_part, g, dh):
    count = len(q)
    key_grads, value_grads = [None] * count, [None] * count
    for t in range(count - 1, -1, -1):
        whole = halves(g, dh)
        minus = c * (carried[t] + exact_times(k[t], whole))
        yield
        value_grads[t] = minus
        g = g + step_back(q[t], k[t], z[t], -minus, dh)
        yield
        partial_grad = key_part[t] - c * full_times(errors[t], whole, nt)
        yield
        key_grads[t] = partial_grad - full_times(minus, halves(weights[t], dh), nt)
        yield
    return key_grads, value_grads, g


def cut(ref, lanes, size=MB):
    return [ref[i : i + size, lanes] for i in range(0, ref.shape[0], size)]


def put(ref, lanes, parts):
    size = ref.shape[0] // len(parts)
    for i, part in enumerate(parts):
        ref[i * size : (i + 1) * size, lanes] = part.astype(ref.dtype)


def kernel(
    dh, width, upstream, q, k, v, rates, checkpoint,
    gq, gk, gv, start,
    rows_of_heads, stage,
    z, trail, err, car, kp, a, b, other_a, other_b, pair_a, pair_b, second_a, second_b,
    entering, leaving, back, end,
    line_sem, up_sems, a_send, a_recv, b_send, b_recv, g_send, g_recv, r_send, r_recv,
):
    shard, shards = lax.axis_index("seq"), lax.axis_size("seq")
    section, sections = lax.axis_index("section"), lax.axis_size("section")
    features = q.shape[1]
    half = features // 2
    chunks = half // width
    side = lax.rem(shard, 2)
    partner = (section, shard + 1 - 2 * side)
    before = (section, jnp.maximum(shard - 2, 0))
    after = (section, jnp.minimum(shard + 2, shards - 1))
    below = (lax.rem(section + sections - 1, sections), shard)
    above = (lax.rem(section + 1, sections), shard)
    not_first = shard >= 2
    not_last = shard < shards - 2

    barrier = pltpu.get_barrier_semaphore()
    for peer in (below, above, partner):
        pl.semaphore_signal(barrier, inc=1, device_id=peer, device_id_type=MESH)
    for present, peer in ((not_first, before), (not_last, after)):
        @pl.when(present)
        def _():
            pl.semaphore_signal(barrier, inc=1, device_id=peer, device_id_type=MESH)
    pl.semaphore_wait(barrier, 3 + not_first.astype(jnp.int32) + not_last.astype(jnp.int32))

    def remote(source, target, send, recv, peer):
        return pltpu.make_async_remote_copy(
            src_ref=source, dst_ref=target, send_sem=send, recv_sem=recv,
            device_id=peer, device_id_type=MESH,
        )

    upward = remote(upstream, z, up_sems.at[0], up_sems.at[1], below)
    upward.start()

    heads = features // dh
    lines = dh * dh // LANES

    def line_in(i):
        return pltpu.make_async_copy(
            checkpoint.at[:, pl.ds(i * LANES, LANES)],
            rows_of_heads.at[pl.ds(i * heads, heads), :],
            line_sem.at[i],
        )

    def line_out(i):
        return pltpu.make_async_copy(
            rows_of_heads.at[pl.ds(i * heads, heads), :],
            start.at[:, pl.ds(i * LANES, LANES)],
            line_sem.at[i],
        )

    for i in range(lines):
        line_in(i).start()
    for i in range(lines):
        line_in(i).wait()

    left = lax.broadcasted_iota(jnp.int32, (lines, LANES), 1) < dh

    def swap(x):
        return jnp.concatenate([x[:, dh:], x[:, :dh]], axis=1)

    def head_of(lanes):
        return (lanes.start // LANES) * (LANES // dh)

    def rate_of(lanes):
        head = head_of(lanes)
        first = lax.broadcasted_iota(jnp.int32, (1, LANES), 1) < dh
        return jnp.where(first, rates[0, head], rates[0, head + 1]) / MB

    def load_weight(lanes):
        head = head_of(lanes)
        x = rows_of_heads[pl.ds(head, lines, stride=heads), :]
        y = rows_of_heads[pl.ds(head + 1, lines, stride=heads), :]
        base = head * (dh // 2)
        stage[pl.ds(base, lines, stride=2), :] = jnp.where(left, x, swap(y))
        stage[pl.ds(base + 1, lines, stride=2), :] = jnp.where(left, swap(x), y)
        trail[:dh, lanes] = stage[pl.ds(pl.multiple_of(base, dh), dh), :]

    def store_start(lanes, first):
        head = head_of(lanes)
        base = head * (dh // 2)
        stage[pl.ds(pl.multiple_of(base, dh), dh), :] = first
        even = stage[pl.ds(base, lines, stride=2), :]
        odd = stage[pl.ds(base + 1, lines, stride=2), :]
        rows_of_heads[pl.ds(head, lines, stride=heads), :] = jnp.where(left, even, swap(odd))
        rows_of_heads[pl.ds(head + 1, lines, stride=heads), :] = jnp.where(left, swap(even), odd)

    def own(i):
        return pl.ds(pl.multiple_of(side * half + i * width, width), width)

    def others(i):
        return pl.ds(pl.multiple_of((1 - side) * half + i * width, width), width)

    def place(i):
        return pl.ds(pl.multiple_of(i * width, width), width)

    def send_a(i):
        return remote(a.at[:, others(i)], other_a.at[:, place(i)], a_send.at[i], a_recv.at[i], partner)

    def send_b(i):
        return remote(b.at[:, others(i)], other_b.at[:, place(i)], b_send.at[i], b_recv.at[i], partner)

    def send_g(i):
        return remote(leaving.at[:, place(i)], entering.at[:, place(i)], g_send.at[i], g_recv.at[i], before)

    def send_r(i):
        return remote(back.at[:, place(i)], end.at[:, own(i)], r_send.at[i], r_recv.at[i], partner)

    def await_r(i):
        return remote(back.at[:, place(i)], end.at[:, others(i)], r_send.at[i], r_recv.at[i], partner)

    def narrow(span):
        start_lane = span.start
        return [
            pl.ds(pl.multiple_of(start_lane + j, LANES), LANES) for j in range(0, width, LANES)
        ]

    def together(compute, store, spans):
        groups = [lanes for span in spans for lanes in narrow(span)]
        results = interleaved([compute(lanes) for lanes in groups])
        for lanes, result in zip(groups, results):
            store(lanes, *result)

    def weights_of(lanes):
        return weight_part(cut(k, lanes), cut(v, lanes), rate_of(lanes), trail[:dh, lanes], dh)

    def put_weights(lanes, weights, errors, linear):
        for t in range(1, len(weights)):
            trail[t * dh : (t + 1) * dh, lanes] = weights[t]
        put(err, lanes, errors)
        a[:, lanes] = linear

    def sources_of(lanes):
        return source_part(cut(q, lanes), cut(k, lanes), cut(z, lanes), rate_of(lanes), dh)

    def put_sources(lanes, carried, offset):
        put(car, lanes, carried)
        b[:, lanes] = offset

    def scores_of(lanes):
        return score_part(
            cut(q, lanes), cut(k, lanes), cut(z, lanes), rate_of(lanes),
            cut(trail, lanes, dh), cut(err, lanes), dh,
        )

    def put_scores(lanes, query_grads, key_part):
        put(gq, lanes, query_grads)
        put(kp, lanes, key_part)

    def finals_of(lanes):
        return final_part(
            cut(q, lanes), cut(k, lanes), cut(z, lanes), rate_of(lanes),
            cut(trail, lanes, dh), cut(err, lanes), cut(car, lanes), cut(kp, lanes), end[:, lanes], dh,
        )

    def put_finals(lanes, key_grads, value_grads, first):
        put(gk, lanes, key_grads)
        put(gv, lanes, value_grads)
        store_start(lanes, first)

    def each(body):
        def step(i, nothing):
            body(i)
            return nothing

        lax.fori_loop(0, chunks, step, jnp.int32(0))

    def first_step(i):
        for span in (others(i), own(i)):
            for lanes in narrow(span):
                load_weight(lanes)
        together(weights_of, put_weights, [others(i), own(i)])
        send_a(i).start()

    def second_step(i):
        together(sources_of, put_sources, [others(i), own(i)])
        send_b(i).start()

    is_even = side == 0

    def pair_step(i):
        lanes, local = own(i), place(i)
        send_a(i).wait_recv()
        send_b(i).wait_recv()
        near_a, near_b = a[:, lanes], b[:, lanes]
        far_a, far_b = other_a[:, local], other_b[:, local]
        a1 = jnp.where(is_even, far_a, near_a)
        b1 = jnp.where(is_even, far_b, near_b)
        a0 = jnp.where(is_even, near_a, far_a)
        b0 = jnp.where(is_even, near_b, far_b)
        offset = full_times(a0, halves(b1, dh)) + b0
        leaving[:, local] = offset

        @pl.when(not_first & jnp.logical_not(not_last))
        def _():
            send_g(i).start()

        pair_b[:, local] = offset
        pair_a[:, local] = full_times(a0, halves(a1, dh))
        second_a[:, local] = a1
        second_b[:, local] = b1

    def relay_step(i):
        lanes, local = own(i), place(i)
        together(scores_of, put_scores, [others(i), lanes])

        @pl.when(not_last)
        def _():
            send_g(i).wait_recv()
            incoming = entering[:, local]
            whole = halves(incoming, dh)
            leaving[:, local] = full_times(pair_a[:, local], whole) + pair_b[:, local]

            @pl.when(not_first)
            def _():
                send_g(i).start()

            middle = full_times(second_a[:, local], whole) + second_b[:, local]
            back[:, local] = jnp.where(is_even, incoming, middle)
            end[:, lanes] = jnp.where(is_even, middle, incoming)

        @pl.when(jnp.logical_not(not_last))
        def _():
            middle = second_b[:, local]
            nothing = jnp.zeros_like(middle)
            back[:, local] = jnp.where(is_even, nothing, middle)
            end[:, lanes] = jnp.where(is_even, middle, nothing)

        send_r(i).start()

    def last_step(i):
        await_r(i).wait_recv()
        together(finals_of, put_finals, [own(i), others(i)])

    def drain(i):
        send_a(i).wait_send()
        send_b(i).wait_send()
        send_r(i).wait_send()

        @pl.when(not_first)
        def _():
            send_g(i).wait_send()

    each(first_step)
    upward.wait_recv()
    each(second_step)
    each(pair_step)
    each(relay_step)
    each(last_step)
    for i in range(lines):
        line_out(i).start()
    each(drain)
    upward.wait_send()
    for i in range(lines):
        line_out(i).wait()


def per_device(queries, memory_keys, memory_values, upstream, inner_rate, checkpoints):
    heads = inner_rate.shape[1]
    features = queries.shape[2]
    dh = features // heads
    tokens = queries.shape[1]
    width = 2 * LANES
    half = features // 2
    chunks = half // width
    count = tokens // MB

    vmem = pl.BlockSpec(memory_space=pltpu.VMEM)
    hbm = pl.BlockSpec(memory_space=pl.ANY)
    assert 2 * dh == LANES
    lines = dh * dh // LANES
    tall = jax.ShapeDtypeStruct((tokens, features), BF16)
    whole = pltpu.VMEM((dh, features), F32)
    part = pltpu.VMEM((dh, half), F32)
    rows = pltpu.VMEM((tokens, features), F32)
    gq, gk, gv, start = pl.pallas_call(
        partial(kernel, dh, width),
        in_specs=[hbm] + [vmem] * 3 + [pl.BlockSpec(memory_space=pltpu.SMEM), hbm],
        out_specs=[vmem] * 3 + [hbm],
        out_shape=[tall, tall, tall, jax.ShapeDtypeStruct((heads, dh * dh), F32)],
        scratch_shapes=[
            pltpu.VMEM((lines * heads, LANES), F32),
            pltpu.VMEM((features // LANES * dh, LANES), F32),
            pltpu.VMEM((tokens, features), BF16),
            pltpu.VMEM((count * dh, features), F32),
            rows, rows, rows,
            whole, whole,
            part, part, part, part, part, part, part, part, part,
            whole,
            pltpu.SemaphoreType.DMA((lines,)),
            pltpu.SemaphoreType.DMA((2,)),
        ] + [pltpu.SemaphoreType.DMA((chunks,))] * 8,
        compiler_params=pltpu.CompilerParams(collective_id=0, has_side_effects=True),
        name="layer_backward",
    )(upstream[0], queries[0], memory_keys[0], memory_values[0], inner_rate, checkpoints[0, 0])
    return gq[None], gk[None], gv[None], start[None, None]


def solution(mesh):
    return jax.shard_map(
        per_device,
        mesh=mesh,
        in_specs=(
            P("section", "seq", None),
            P("section", "seq", None),
            P("section", "seq", None),
            P("section", "seq", None),
            P("section", None),
            P("section", "seq", None, None),
        ),
        out_specs=(
            P("section", "seq", None),
            P("section", "seq", None),
            P("section", "seq", None),
            P("section", "seq", None, None),
        ),
        check_vma=False,
    )
```

```python
from functools import partial

import jax
import jax.numpy as jnp
from jax import lax
from jax.experimental import pallas as pl
from jax.experimental.pallas import tpu as pltpu
from jax.sharding import PartitionSpec as P

MB = 64
LANES = 128
F32 = jnp.float32
BF16 = jnp.bfloat16
MESH = pl.DeviceIdType.MESH


def nn(a, b):
    return lax.dot_general(a, b, (((1,), (0,)), ((), ())), preferred_element_type=F32)


def nt(a, b):
    return lax.dot_general(a, b, (((1,), (1,)), ((), ())), preferred_element_type=F32)


def tn(a, b):
    return lax.dot_general(a, b, (((0,), (0,)), ((), ())), preferred_element_type=F32)


def split(x):
    high = x.astype(BF16)
    return high, (x - high.astype(F32)).astype(BF16)


def stacked(parts):
    return jnp.concatenate(parts, axis=0)


def tiles(x):
    return [x[:, i : i + LANES] for i in range(0, x.shape[1], LANES)]


def diagonal(x, dh):
    per = LANES // dh
    lane = lax.broadcasted_iota(jnp.int32, (x.shape[0], LANES), 1) // dh
    masks = [(lane == i).astype(F32).astype(BF16) for i in range(per)]
    pieces = tiles(x)
    zero = jnp.zeros((x.shape[0], LANES), x.dtype)
    rows = []
    for t, piece in enumerate(pieces):
        for i in range(per):
            row = [zero] * len(pieces)
            row[t] = piece * masks[i]
            rows.append(jnp.concatenate(row, axis=1))
    return stacked(rows)


def folded(a, b, dh):
    per = LANES // dh
    lane = lax.broadcasted_iota(jnp.int32, (dh, LANES), 1) // dh
    out = []
    for left, right in zip(tiles(a), tiles(b)):
        product = tn(left, right)
        value = product[:dh]
        for i in range(1, per):
            value = jnp.where(lane == i, product[i * dh : (i + 1) * dh], value)
        out.append(value)
    return jnp.concatenate(out, axis=1)


def rows_times(x, weights, multiply=nn):
    high, low = split(x)
    both = multiply(stacked([high, low]), weights)
    return both[: x.shape[0]] + both[x.shape[0] :]


def full_times(x, weights, multiply=nn):
    return rows_times(x, weights[0], multiply) + multiply(x.astype(BF16), weights[1])


def halves(x, dh):
    high, low = split(x)
    return diagonal(high, dh), diagonal(low, dh)


def exact_times(x, weights, multiply=nn):
    return multiply(x, weights[0]) + multiply(x, weights[1])


def doubled(a, b):
    return stacked([a, a]), stacked(split(b))


def lane_index(shape, dh):
    return lax.broadcasted_iota(jnp.int32, shape, 1) % dh


def upper_mask(width):
    row = lax.broadcasted_iota(jnp.int32, (MB, width), 0)
    return (lane_index((MB, width), MB) >= row).astype(F32)


def weight_part(k, v, c, w, dh):
    width = c.shape[1]
    row = lax.broadcasted_iota(jnp.int32, (dh, width), 0)
    eye = jnp.where(row == lane_index((dh, width), dh), 1.0, 0.0)
    weights, errors, linear = [], [], []
    for t in range(len(k)):
        e = exact_times(k[t], halves(w, dh)) - v[t].astype(F32)
        yield
        weights.append(w)
        errors.append(e)
        if t + 1 < len(k):
            w = w - c * folded(*doubled(k[t], e), dh)
            yield
        linear.append(eye - c * folded(k[t], k[t], dh))
        yield
    a = linear[-1]
    for t in range(len(k) - 2, -1, -1):
        a = full_times(linear[t], halves(a, dh))
    return weights, errors, a


def interleaved(runs):
    results, waiting = [None] * len(runs), dict(enumerate(runs))
    while waiting:
        for i, run in list(waiting.items()):
            try:
                next(run)
            except StopIteration as stop:
                results[i] = stop.value
                del waiting[i]
    return results


def step_back(q, k, z, error_grad, dh):
    high, low = split(error_grad)
    return folded(stacked([q, k, k]), stacked([z, high, low]), dh)


def source_part(q, k, z, c, dh):
    upper = upper_mask(c.shape[1])
    carried = [None] * len(k)
    for t in range(len(k) - 1, -1, -1):
        scores = nt(k[t], diagonal(q[t], dh)) * upper
        yield
        carried[t] = rows_times(scores, diagonal(z[t], dh))
        yield
    b = None
    for t in range(len(k) - 1, -1, -1):
        total = carried[t] if b is None else carried[t] + exact_times(k[t], halves(b, dh))
        yield
        update = step_back(q[t], k[t], z[t], total * -c, dh)
        b = update if b is None else b + update
        yield
    return carried, b


def score_part(q, k, z, c, weights, errors, dh):
    upper = upper_mask(c.shape[1])
    query_grads, key_part = [], []
    for t in range(len(k)):
        score_grad = rows_times(errors[t], diagonal(z[t], dh), nt) * (upper * -c)
        yield
        key_part.append(rows_times(score_grad, diagonal(q[t], dh)))
        yield
        high, low = split(score_grad)
        query_grads.append(
            exact_times(z[t], halves(weights[t], dh), nt)
            + folded(stacked([high, low]), stacked([k[t], k[t]]), dh)
        )
        yield
    return query_grads, key_part


def final_part(q, k, z, c, weights, errors, carried, key_part, g, dh):
    count = len(q)
    key_grads, value_grads = [None] * count, [None] * count
    for t in range(count - 1, -1, -1):
        whole = halves(g, dh)
        minus = c * (carried[t] + exact_times(k[t], whole))
        yield
        value_grads[t] = minus
        g = g + step_back(q[t], k[t], z[t], -minus, dh)
        yield
        partial_grad = key_part[t] - c * full_times(errors[t], whole, nt)
        yield
        key_grads[t] = partial_grad - full_times(minus, halves(weights[t], dh), nt)
        yield
    return key_grads, value_grads, g


def cut(ref, lanes, size=MB):
    return [ref[i : i + size, lanes] for i in range(0, ref.shape[0], size)]


def put(ref, lanes, parts):
    size = ref.shape[0] // len(parts)
    for i, part in enumerate(parts):
        ref[i * size : (i + 1) * size, lanes] = part.astype(ref.dtype)


def kernel(
    dh, width, upstream, q, k, v, rates, checkpoint,
    gq, gk, gv, rows_of_heads,
    stage,
    z, trail, err, car, kp, a, b, other_a, other_b, pair_a, pair_b, second_a, second_b,
    entering, leaving, back, end,
    line_sem, up_sems, a_send, a_recv, b_send, b_recv, g_send, g_recv, r_send, r_recv,
):
    shard, shards = lax.axis_index("seq"), lax.axis_size("seq")
    section, sections = lax.axis_index("section"), lax.axis_size("section")
    features = q.shape[1]
    half = features // 2
    chunks = half // width
    side = lax.rem(shard, 2)
    partner = (section, shard + 1 - 2 * side)
    before = (section, jnp.maximum(shard - 2, 0))
    after = (section, jnp.minimum(shard + 2, shards - 1))
    below = (lax.rem(section + sections - 1, sections), shard)
    above = (lax.rem(section + 1, sections), shard)
    not_first = shard >= 2
    not_last = shard < shards - 2

    barrier = pltpu.get_barrier_semaphore()
    for peer in (below, above, partner):
        pl.semaphore_signal(barrier, inc=1, device_id=peer, device_id_type=MESH)
    for present, peer in ((not_first, before), (not_last, after)):
        @pl.when(present)
        def _():
            pl.semaphore_signal(barrier, inc=1, device_id=peer, device_id_type=MESH)
    pl.semaphore_wait(barrier, 3 + not_first.astype(jnp.int32) + not_last.astype(jnp.int32))

    def remote(source, target, send, recv, peer):
        return pltpu.make_async_remote_copy(
            src_ref=source, dst_ref=target, send_sem=send, recv_sem=recv,
            device_id=peer, device_id_type=MESH,
        )

    upward = remote(upstream, z, up_sems.at[0], up_sems.at[1], below)
    upward.start()

    heads = features // dh
    lines = dh * dh // LANES

    def line_in(i):
        return pltpu.make_async_copy(
            checkpoint.at[:, pl.ds(i * LANES, LANES)],
            rows_of_heads.at[pl.ds(i * heads, heads), :],
            line_sem.at[i],
        )

    for i in range(lines):
        line_in(i).start()
    for i in range(lines):
        line_in(i).wait()

    left = lax.broadcasted_iota(jnp.int32, (lines, LANES), 1) < dh

    def swap(x):
        return jnp.concatenate([x[:, dh:], x[:, :dh]], axis=1)

    def head_of(lanes):
        return (lanes.start // LANES) * (LANES // dh)

    def rate_of(lanes):
        head = head_of(lanes)
        first = lax.broadcasted_iota(jnp.int32, (1, LANES), 1) < dh
        return jnp.where(first, rates[0, head], rates[0, head + 1]) / MB

    def load_weight(lanes):
        head = head_of(lanes)
        x = rows_of_heads[pl.ds(head, lines, stride=heads), :]
        y = rows_of_heads[pl.ds(head + 1, lines, stride=heads), :]
        base = head * (dh // 2)
        stage[pl.ds(base, lines, stride=2), :] = jnp.where(left, x, swap(y))
        stage[pl.ds(base + 1, lines, stride=2), :] = jnp.where(left, swap(x), y)
        trail[:dh, lanes] = stage[pl.ds(pl.multiple_of(base, dh), dh), :]

    def store_start(lanes, first):
        head = head_of(lanes)
        base = head * (dh // 2)
        stage[pl.ds(pl.multiple_of(base, dh), dh), :] = first
        even = stage[pl.ds(base, lines, stride=2), :]
        odd = stage[pl.ds(base + 1, lines, stride=2), :]
        rows_of_heads[pl.ds(head, lines, stride=heads), :] = jnp.where(left, even, swap(odd))
        rows_of_heads[pl.ds(head + 1, lines, stride=heads), :] = jnp.where(left, swap(even), odd)

    def own(i):
        return pl.ds(pl.multiple_of(side * half + i * width, width), width)

    def others(i):
        return pl.ds(pl.multiple_of((1 - side) * half + i * width, width), width)

    def place(i):
        return pl.ds(pl.multiple_of(i * width, width), width)

    def send_a(i):
        return remote(a.at[:, others(i)], other_a.at[:, place(i)], a_send.at[i], a_recv.at[i], partner)

    def send_b(i):
        return remote(b.at[:, others(i)], other_b.at[:, place(i)], b_send.at[i], b_recv.at[i], partner)

    def thin(i):
        return pl.ds(pl.multiple_of(i * LANES, LANES), LANES)

    def own_thin(i):
        return pl.ds(pl.multiple_of(side * half + i * LANES, LANES), LANES)

    def others_thin(i):
        return pl.ds(pl.multiple_of((1 - side) * half + i * LANES, LANES), LANES)

    fine = width // LANES

    def send_g(i):
        return remote(leaving.at[:, thin(i)], entering.at[:, thin(i)], g_send.at[i], g_recv.at[i], before)

    def send_r(i):
        return remote(back.at[:, thin(i)], end.at[:, own_thin(i)], r_send.at[i], r_recv.at[i], partner)

    def await_r(i):
        return remote(back.at[:, thin(i)], end.at[:, others_thin(i)], r_send.at[i], r_recv.at[i], partner)

    def narrow(span):
        start_lane = span.start
        return [
            pl.ds(pl.multiple_of(start_lane + j, LANES), LANES) for j in range(0, width, LANES)
        ]

    def together(compute, store, spans):
        groups = [lanes for span in spans for lanes in narrow(span)]
        results = interleaved([compute(lanes) for lanes in groups])
        for lanes, result in zip(groups, results):
            store(lanes, *result)

    def weights_of(lanes):
        return weight_part(cut(k, lanes), cut(v, lanes), rate_of(lanes), trail[:dh, lanes], dh)

    def put_weights(lanes, weights, errors, linear):
        for t in range(1, len(weights)):
            trail[t * dh : (t + 1) * dh, lanes] = weights[t]
        put(err, lanes, errors)
        a[:, lanes] = linear

    def sources_of(lanes):
        return source_part(cut(q, lanes), cut(k, lanes), cut(z, lanes), rate_of(lanes), dh)

    def put_sources(lanes, carried, offset):
        put(car, lanes, carried)
        b[:, lanes] = offset

    def scores_of(lanes):
        return score_part(
            cut(q, lanes), cut(k, lanes), cut(z, lanes), rate_of(lanes),
            cut(trail, lanes, dh), cut(err, lanes), dh,
        )

    def put_scores(lanes, query_grads, key_part):
        put(gq, lanes, query_grads)
        put(kp, lanes, key_part)

    def finals_of(lanes):
        return final_part(
            cut(q, lanes), cut(k, lanes), cut(z, lanes), rate_of(lanes),
            cut(trail, lanes, dh), cut(err, lanes), cut(car, lanes), cut(kp, lanes), end[:, lanes], dh,
        )

    def put_finals(lanes, key_grads, value_grads, first):
        put(gk, lanes, key_grads)
        put(gv, lanes, value_grads)
        store_start(lanes, first)

    def each(body, first=0, last=chunks):
        def step(i, nothing):
            body(i)
            return nothing

        lax.fori_loop(first, last, step, jnp.int32(0))

    def first_step(i):
        for span in (others(i), own(i)):
            for lanes in narrow(span):
                load_weight(lanes)
        together(weights_of, put_weights, [others(i), own(i)])
        send_a(i).start()

    def second_step(i):
        together(sources_of, put_sources, [others(i), own(i)])
        send_b(i).start()

    is_even = side == 0

    def pair_step(i):
        lanes, local = own(i), place(i)
        send_a(i).wait_recv()
        send_b(i).wait_recv()
        near_a, near_b = a[:, lanes], b[:, lanes]
        far_a, far_b = other_a[:, local], other_b[:, local]
        a1 = jnp.where(is_even, far_a, near_a)
        b1 = jnp.where(is_even, far_b, near_b)
        a0 = jnp.where(is_even, near_a, far_a)
        b0 = jnp.where(is_even, near_b, far_b)
        offset = full_times(a0, halves(b1, dh)) + b0
        leaving[:, local] = offset

        @pl.when(not_first & jnp.logical_not(not_last))
        def _():
            for j in range(fine):
                send_g(i * fine + j).start()

        pair_b[:, local] = offset
        pair_a[:, local] = full_times(a0, halves(a1, dh))
        second_a[:, local] = a1
        second_b[:, local] = b1

    def score_step(i):
        together(scores_of, put_scores, [others(i), own(i)])

    def relay_step(i):
        lanes, local = own_thin(i), thin(i)

        @pl.when(not_last)
        def _():
            send_g(i).wait_recv()
            incoming = entering[:, local]
            whole = halves(incoming, dh)
            leaving[:, local] = full_times(pair_a[:, local], whole) + pair_b[:, local]

            @pl.when(not_first)
            def _():
                send_g(i).start()

            middle = full_times(second_a[:, local], whole) + second_b[:, local]
            back[:, local] = jnp.where(is_even, incoming, middle)
            end[:, lanes] = jnp.where(is_even, middle, incoming)

        @pl.when(jnp.logical_not(not_last))
        def _():
            middle = second_b[:, local]
            nothing = jnp.zeros_like(middle)
            back[:, local] = jnp.where(is_even, nothing, middle)
            end[:, lanes] = jnp.where(is_even, middle, nothing)

        send_r(i).start()

    def last_step(i):
        for j in range(fine):
            await_r(i * fine + j).wait_recv()
        together(finals_of, put_finals, [own(i), others(i)])

    def drain(i):
        send_a(i).wait_send()
        send_b(i).wait_send()
        for j in range(fine):
            send_r(i * fine + j).wait_send()

            @pl.when(not_first)
            def _():
                send_g(i * fine + j).wait_send()

    each(first_step)
    upward.wait_recv()
    each(second_step)
    each(pair_step)
    early = jnp.where(shard < shards - 4, chunks, 0)
    each(score_step, 0, early)
    each(relay_step, 0, chunks * fine)
    each(score_step, early, chunks)
    each(last_step)
    each(drain)
    upward.wait_send()


def store_kernel(heads, gq, gk, gv, rows, gq_out, gk_out, gv_out, start_out, sems, line_sem):
    copies = [
        pltpu.make_async_copy(
            rows.at[pl.ds(i * heads, heads), :], start_out.at[:, pl.ds(i * LANES, LANES)], line_sem.at[i]
        )
        for i in range(rows.shape[0] // heads)
    ] + [
        pltpu.make_async_copy(x, y, sems.at[i])
        for i, (x, y) in enumerate(((gq, gq_out), (gk, gk_out), (gv, gv_out)))
    ]
    for copy in copies:
        copy.start()
    for copy in copies:
        copy.wait()


def per_device(queries, memory_keys, memory_values, upstream, inner_rate, checkpoints):
    heads = inner_rate.shape[1]
    features = queries.shape[2]
    dh = features // heads
    tokens = queries.shape[1]
    width = 2 * LANES
    half = features // 2
    chunks = half // width
    count = tokens // MB

    vmem = pl.BlockSpec(memory_space=pltpu.VMEM)
    hbm = pl.BlockSpec(memory_space=pl.ANY)
    assert 2 * dh == LANES
    lines = dh * dh // LANES
    tall = jax.ShapeDtypeStruct((tokens, features), BF16)
    held = pltpu.VMEM((tokens, features), BF16)
    whole = pltpu.VMEM((dh, features), F32)
    part = pltpu.VMEM((dh, half), F32)
    rows = pltpu.VMEM((tokens, features), F32)
    gq, gk, gv, start_rows = pl.pallas_call(
        partial(kernel, dh, width),
        in_specs=[hbm] + [vmem] * 3 + [pl.BlockSpec(memory_space=pltpu.SMEM), hbm],
        out_specs=[vmem] * 4,
        out_shape=[held, held, held, pltpu.VMEM((lines * heads, LANES), F32)],
        scratch_shapes=[
            pltpu.VMEM((features // LANES * dh, LANES), F32),
            pltpu.VMEM((tokens, features), BF16),
            pltpu.VMEM((count * dh, features), F32),
            rows, rows, rows,
            whole, whole,
            part, part, part, part, part, part, part, part, part,
            whole,
            pltpu.SemaphoreType.DMA((lines,)),
            pltpu.SemaphoreType.DMA((2,)),
        ] + [pltpu.SemaphoreType.DMA((chunks,))] * 4
        + [pltpu.SemaphoreType.DMA((half // LANES,))] * 4,
        compiler_params=pltpu.CompilerParams(collective_id=0, has_side_effects=True, vmem_limit_bytes=40 * 2**20),
        name="layer_backward",
    )(upstream[0], queries[0], memory_keys[0], memory_values[0], inner_rate, checkpoints[0, 0])
    gq, gk, gv, start = pl.pallas_call(
        partial(store_kernel, heads),
        in_specs=[hbm] * 4,
        out_specs=[hbm] * 4,
        out_shape=[tall, tall, tall, jax.ShapeDtypeStruct((heads, dh * dh), F32)],
        scratch_shapes=[pltpu.SemaphoreType.DMA((3,)), pltpu.SemaphoreType.DMA((lines,))],
        compiler_params=pltpu.CompilerParams(vmem_limit_bytes=2**20),
        name="store_results",
    )(gq, gk, gv, start_rows)
    return gq[None], gk[None], gv[None], start[None, None]


def solution(mesh):
    return jax.shard_map(
        per_device,
        mesh=mesh,
        in_specs=(
            P("section", "seq", None),
            P("section", "seq", None),
            P("section", "seq", None),
            P("section", "seq", None),
            P("section", None),
            P("section", "seq", None, None),
        ),
        out_specs=(
            P("section", "seq", None),
            P("section", "seq", None),
            P("section", "seq", None),
            P("section", "seq", None, None),
        ),
        check_vma=False,
    )
```

```python
from functools import partial

import jax
import jax.numpy as jnp
from jax import lax
from jax.experimental import pallas as pl
from jax.experimental.pallas import tpu as pltpu
from jax.sharding import PartitionSpec as P

MB = 64
LANES = 128
F32 = jnp.float32
BF16 = jnp.bfloat16
MESH = pl.DeviceIdType.MESH


def nn(a, b):
    return lax.dot_general(a, b, (((1,), (0,)), ((), ())), preferred_element_type=F32)


def nt(a, b):
    return lax.dot_general(a, b, (((1,), (1,)), ((), ())), preferred_element_type=F32)


def tn(a, b):
    return lax.dot_general(a, b, (((0,), (0,)), ((), ())), preferred_element_type=F32)


def split(x):
    high = x.astype(BF16)
    return high, (x - high.astype(F32)).astype(BF16)


def stacked(parts):
    return jnp.concatenate(parts, axis=0)


def tiles(x):
    return [x[:, i : i + LANES] for i in range(0, x.shape[1], LANES)]


def diagonal(x, dh):
    per = LANES // dh
    lane = lax.broadcasted_iota(jnp.int32, (x.shape[0], LANES), 1) // dh
    masks = [(lane == i).astype(F32).astype(BF16) for i in range(per)]
    pieces = tiles(x)
    zero = jnp.zeros((x.shape[0], LANES), x.dtype)
    rows = []
    for t, piece in enumerate(pieces):
        for i in range(per):
            row = [zero] * len(pieces)
            row[t] = piece * masks[i]
            rows.append(jnp.concatenate(row, axis=1))
    return stacked(rows)


def folded(a, b, dh):
    per = LANES // dh
    lane = lax.broadcasted_iota(jnp.int32, (dh, LANES), 1) // dh
    out = []
    for left, right in zip(tiles(a), tiles(b)):
        product = tn(left, right)
        value = product[:dh]
        for i in range(1, per):
            value = jnp.where(lane == i, product[i * dh : (i + 1) * dh], value)
        out.append(value)
    return jnp.concatenate(out, axis=1)


def rows_times(x, weights, multiply=nn):
    high, low = split(x)
    both = multiply(stacked([high, low]), weights)
    return both[: x.shape[0]] + both[x.shape[0] :]


def full_times(x, weights, multiply=nn):
    return rows_times(x, weights[0], multiply) + multiply(x.astype(BF16), weights[1])


def halves(x, dh):
    high, low = split(x)
    return diagonal(high, dh), diagonal(low, dh)


def exact_times(x, weights, multiply=nn):
    return multiply(x, weights[0]) + multiply(x, weights[1])


def doubled(a, b):
    return stacked([a, a]), stacked(split(b))


def lane_index(shape, dh):
    return lax.broadcasted_iota(jnp.int32, shape, 1) % dh


def upper_mask(width):
    row = lax.broadcasted_iota(jnp.int32, (MB, width), 0)
    return (lane_index((MB, width), MB) >= row).astype(F32)


def weight_part(k, v, c, w, dh):
    width = c.shape[1]
    row = lax.broadcasted_iota(jnp.int32, (dh, width), 0)
    eye = jnp.where(row == lane_index((dh, width), dh), 1.0, 0.0)
    weights, errors, linear = [], [], []
    for t in range(len(k)):
        e = exact_times(k[t], halves(w, dh)) - v[t].astype(F32)
        yield
        weights.append(w)
        errors.append(e)
        if t + 1 < len(k):
            w = w - c * folded(*doubled(k[t], e), dh)
            yield
        linear.append(eye - c * folded(k[t], k[t], dh))
        yield
    a = linear[-1]
    for t in range(len(k) - 2, -1, -1):
        a = full_times(linear[t], halves(a, dh))
    return weights, errors, a


def interleaved(runs):
    results, waiting = [None] * len(runs), dict(enumerate(runs))
    while waiting:
        for i, run in list(waiting.items()):
            try:
                next(run)
            except StopIteration as stop:
                results[i] = stop.value
                del waiting[i]
    return results


def step_back(q, k, z, error_grad, dh):
    high, low = split(error_grad)
    return folded(stacked([q, k, k]), stacked([z, high, low]), dh)


def source_part(q, k, z, c, dh):
    upper = upper_mask(c.shape[1])
    carried = [None] * len(k)
    for t in range(len(k) - 1, -1, -1):
        scores = nt(k[t], diagonal(q[t], dh)) * upper
        yield
        carried[t] = rows_times(scores, diagonal(z[t], dh))
        yield
    b = None
    for t in range(len(k) - 1, -1, -1):
        total = carried[t] if b is None else carried[t] + exact_times(k[t], halves(b, dh))
        yield
        update = step_back(q[t], k[t], z[t], total * -c, dh)
        b = update if b is None else b + update
        yield
    return carried, b


def score_part(q, k, z, c, weights, errors, dh):
    upper = upper_mask(c.shape[1])
    query_grads, key_part = [], []
    for t in range(len(k)):
        score_grad = rows_times(errors[t], diagonal(z[t], dh), nt) * (upper * -c)
        yield
        key_part.append(rows_times(score_grad, diagonal(q[t], dh)))
        yield
        high, low = split(score_grad)
        query_grads.append(
            exact_times(z[t], halves(weights[t], dh), nt)
            + folded(stacked([high, low]), stacked([k[t], k[t]]), dh)
        )
        yield
    return query_grads, key_part


def final_part(q, k, z, c, weights, errors, carried, key_part, g, dh):
    count = len(q)
    key_grads, value_grads = [None] * count, [None] * count
    for t in range(count - 1, -1, -1):
        whole = halves(g, dh)
        minus = c * (carried[t] + exact_times(k[t], whole))
        yield
        value_grads[t] = minus
        g = g + step_back(q[t], k[t], z[t], -minus, dh)
        yield
        partial_grad = key_part[t] - c * full_times(errors[t], whole, nt)
        yield
        key_grads[t] = partial_grad - full_times(minus, halves(weights[t], dh), nt)
        yield
    return key_grads, value_grads, g


def cut(ref, lanes, size=MB):
    return [ref[i : i + size, lanes] for i in range(0, ref.shape[0], size)]


def put(ref, lanes, parts):
    size = ref.shape[0] // len(parts)
    for i, part in enumerate(parts):
        ref[i * size : (i + 1) * size, lanes] = part.astype(ref.dtype)


def kernel(
    dh, width, upstream, q_in, k_in, v_in, rates, checkpoint,
    gq, gk, gv, rows_of_heads,
    q, k, v, in_sems, stage,
    z, trail, err, car, kp, a, b, other_a, other_b, pair_a, pair_b, second_a, second_b,
    entering, leaving, back, end,
    line_sem, up_sems, a_send, a_recv, b_send, b_recv, g_send, g_recv, r_send, r_recv,
):
    shard, shards = lax.axis_index("seq"), lax.axis_size("seq")
    section, sections = lax.axis_index("section"), lax.axis_size("section")
    features = q.shape[1]
    half = features // 2
    chunks = half // width
    side = lax.rem(shard, 2)
    partner = (section, shard + 1 - 2 * side)
    before = (section, jnp.maximum(shard - 2, 0))
    after = (section, jnp.minimum(shard + 2, shards - 1))
    below = (lax.rem(section + sections - 1, sections), shard)
    above = (lax.rem(section + 1, sections), shard)
    not_first = shard >= 2
    not_last = shard < shards - 2

    loads = [
        pltpu.make_async_copy(x, y, in_sems.at[i])
        for i, (x, y) in enumerate(((k_in, k), (v_in, v), (q_in, q)))
    ]
    for load in loads:
        load.start()

    barrier = pltpu.get_barrier_semaphore()
    for peer in (below, above, partner):
        pl.semaphore_signal(barrier, inc=1, device_id=peer, device_id_type=MESH)
    for present, peer in ((not_first, before), (not_last, after)):
        @pl.when(present)
        def _():
            pl.semaphore_signal(barrier, inc=1, device_id=peer, device_id_type=MESH)
    pl.semaphore_wait(barrier, 3 + not_first.astype(jnp.int32) + not_last.astype(jnp.int32))

    def remote(source, target, send, recv, peer):
        return pltpu.make_async_remote_copy(
            src_ref=source, dst_ref=target, send_sem=send, recv_sem=recv,
            device_id=peer, device_id_type=MESH,
        )

    upward = remote(upstream, z, up_sems.at[0], up_sems.at[1], below)
    upward.start()

    heads = features // dh
    lines = dh * dh // LANES

    def line_in(i):
        return pltpu.make_async_copy(
            checkpoint.at[:, pl.ds(i * LANES, LANES)],
            rows_of_heads.at[pl.ds(i * heads, heads), :],
            line_sem.at[i],
        )

    for i in range(lines):
        line_in(i).start()
    for i in range(lines):
        line_in(i).wait()

    left = lax.broadcasted_iota(jnp.int32, (lines, LANES), 1) < dh

    def swap(x):
        return jnp.concatenate([x[:, dh:], x[:, :dh]], axis=1)

    def head_of(lanes):
        return (lanes.start // LANES) * (LANES // dh)

    def rate_of(lanes):
        head = head_of(lanes)
        first = lax.broadcasted_iota(jnp.int32, (1, LANES), 1) < dh
        return jnp.where(first, rates[0, head], rates[0, head + 1]) / MB

    def load_weight(lanes):
        head = head_of(lanes)
        x = rows_of_heads[pl.ds(head, lines, stride=heads), :]
        y = rows_of_heads[pl.ds(head + 1, lines, stride=heads), :]
        base = head * (dh // 2)
        stage[pl.ds(base, lines, stride=2), :] = jnp.where(left, x, swap(y))
        stage[pl.ds(base + 1, lines, stride=2), :] = jnp.where(left, swap(x), y)
        trail[:dh, lanes] = stage[pl.ds(pl.multiple_of(base, dh), dh), :]

    def store_start(lanes, first):
        head = head_of(lanes)
        base = head * (dh // 2)
        stage[pl.ds(pl.multiple_of(base, dh), dh), :] = first
        even = stage[pl.ds(base, lines, stride=2), :]
        odd = stage[pl.ds(base + 1, lines, stride=2), :]
        rows_of_heads[pl.ds(head, lines, stride=heads), :] = jnp.where(left, even, swap(odd))
        rows_of_heads[pl.ds(head + 1, lines, stride=heads), :] = jnp.where(left, swap(even), odd)

    def own(i):
        return pl.ds(pl.multiple_of(side * half + i * width, width), width)

    def others(i):
        return pl.ds(pl.multiple_of((1 - side) * half + i * width, width), width)

    def place(i):
        return pl.ds(pl.multiple_of(i * width, width), width)

    def send_a(i):
        return remote(a.at[:, others(i)], other_a.at[:, place(i)], a_send.at[i], a_recv.at[i], partner)

    def send_b(i):
        return remote(b.at[:, others(i)], other_b.at[:, place(i)], b_send.at[i], b_recv.at[i], partner)

    def thin(i):
        return pl.ds(pl.multiple_of(i * LANES, LANES), LANES)

    def own_thin(i):
        return pl.ds(pl.multiple_of(side * half + i * LANES, LANES), LANES)

    def others_thin(i):
        return pl.ds(pl.multiple_of((1 - side) * half + i * LANES, LANES), LANES)

    fine = width // LANES

    def send_g(i):
        return remote(leaving.at[:, thin(i)], entering.at[:, thin(i)], g_send.at[i], g_recv.at[i], before)

    def send_r(i):
        return remote(back.at[:, thin(i)], end.at[:, own_thin(i)], r_send.at[i], r_recv.at[i], partner)

    def await_r(i):
        return remote(back.at[:, thin(i)], end.at[:, others_thin(i)], r_send.at[i], r_recv.at[i], partner)

    def narrow(span):
        start_lane = span.start
        return [
            pl.ds(pl.multiple_of(start_lane + j, LANES), LANES) for j in range(0, width, LANES)
        ]

    def together(compute, store, spans):
        groups = [lanes for span in spans for lanes in narrow(span)]
        results = interleaved([compute(lanes) for lanes in groups])
        for lanes, result in zip(groups, results):
            store(lanes, *result)

    def weights_of(lanes):
        return weight_part(cut(k, lanes), cut(v, lanes), rate_of(lanes), trail[:dh, lanes], dh)

    def put_weights(lanes, weights, errors, linear):
        for t in range(1, len(weights)):
            trail[t * dh : (t + 1) * dh, lanes] = weights[t]
        put(err, lanes, errors)
        a[:, lanes] = linear

    def sources_of(lanes):
        return source_part(cut(q, lanes), cut(k, lanes), cut(z, lanes), rate_of(lanes), dh)

    def put_sources(lanes, carried, offset):
        put(car, lanes, carried)
        b[:, lanes] = offset

    def scores_of(lanes):
        return score_part(
            cut(q, lanes), cut(k, lanes), cut(z, lanes), rate_of(lanes),
            cut(trail, lanes, dh), cut(err, lanes), dh,
        )

    def put_scores(lanes, query_grads, key_part):
        put(gq, lanes, query_grads)
        put(kp, lanes, key_part)

    def finals_of(lanes):
        return final_part(
            cut(q, lanes), cut(k, lanes), cut(z, lanes), rate_of(lanes),
            cut(trail, lanes, dh), cut(err, lanes), cut(car, lanes), cut(kp, lanes), end[:, lanes], dh,
        )

    def put_finals(lanes, key_grads, value_grads, first):
        put(gk, lanes, key_grads)
        put(gv, lanes, value_grads)
        store_start(lanes, first)

    def each(body, first=0, last=chunks):
        def step(i, nothing):
            body(i)
            return nothing

        lax.fori_loop(first, last, step, jnp.int32(0))

    def first_step(i):
        for span in (others(i), own(i)):
            for lanes in narrow(span):
                load_weight(lanes)
        together(weights_of, put_weights, [others(i), own(i)])
        send_a(i).start()

    def second_step(i):
        together(sources_of, put_sources, [others(i), own(i)])
        send_b(i).start()

    is_even = side == 0

    def pair_step(i):
        lanes, local = own(i), place(i)
        send_a(i).wait_recv()
        send_b(i).wait_recv()
        near_a, near_b = a[:, lanes], b[:, lanes]
        far_a, far_b = other_a[:, local], other_b[:, local]
        a1 = jnp.where(is_even, far_a, near_a)
        b1 = jnp.where(is_even, far_b, near_b)
        a0 = jnp.where(is_even, near_a, far_a)
        b0 = jnp.where(is_even, near_b, far_b)
        offset = full_times(a0, halves(b1, dh)) + b0
        leaving[:, local] = offset

        @pl.when(not_first & jnp.logical_not(not_last))
        def _():
            for j in range(fine):
                send_g(i * fine + j).start()

        pair_b[:, local] = offset
        pair_a[:, local] = full_times(a0, halves(a1, dh))
        second_a[:, local] = a1
        second_b[:, local] = b1

    def score_step(i):
        together(scores_of, put_scores, [others(i), own(i)])

    def relay_step(i):
        lanes, local = own_thin(i), thin(i)

        @pl.when(not_last)
        def _():
            send_g(i).wait_recv()
            incoming = entering[:, local]
            whole = halves(incoming, dh)
            leaving[:, local] = full_times(pair_a[:, local], whole) + pair_b[:, local]

            @pl.when(not_first)
            def _():
                send_g(i).start()

            middle = full_times(second_a[:, local], whole) + second_b[:, local]
            back[:, local] = jnp.where(is_even, incoming, middle)
            end[:, lanes] = jnp.where(is_even, middle, incoming)

        @pl.when(jnp.logical_not(not_last))
        def _():
            middle = second_b[:, local]
            nothing = jnp.zeros_like(middle)
            back[:, local] = jnp.where(is_even, nothing, middle)
            end[:, lanes] = jnp.where(is_even, middle, nothing)

        send_r(i).start()

    def last_step(i):
        for j in range(fine):
            await_r(i * fine + j).wait_recv()
        together(finals_of, put_finals, [own(i), others(i)])

    def drain(i):
        send_a(i).wait_send()
        send_b(i).wait_send()
        for j in range(fine):
            send_r(i * fine + j).wait_send()

            @pl.when(not_first)
            def _():
                send_g(i * fine + j).wait_send()

    loads[0].wait()
    loads[1].wait()
    each(first_step)
    loads[2].wait()
    upward.wait_recv()
    each(second_step)
    each(pair_step)
    early = jnp.where(shard < shards - 4, chunks, 0)
    each(score_step, 0, early)
    each(relay_step, 0, chunks * fine)
    each(score_step, early, chunks)
    each(last_step)
    each(drain)
    upward.wait_send()


def store_kernel(heads, gq, gk, gv, rows, gq_out, gk_out, gv_out, start_out, sems, line_sem):
    copies = [
        pltpu.make_async_copy(
            rows.at[pl.ds(i * heads, heads), :], start_out.at[:, pl.ds(i * LANES, LANES)], line_sem.at[i]
        )
        for i in range(rows.shape[0] // heads)
    ] + [
        pltpu.make_async_copy(x, y, sems.at[i])
        for i, (x, y) in enumerate(((gq, gq_out), (gk, gk_out), (gv, gv_out)))
    ]
    for copy in copies:
        copy.start()
    for copy in copies:
        copy.wait()


def per_device(queries, memory_keys, memory_values, upstream, inner_rate, checkpoints):
    heads = inner_rate.shape[1]
    features = queries.shape[2]
    dh = features // heads
    tokens = queries.shape[1]
    width = 2 * LANES
    half = features // 2
    chunks = half // width
    count = tokens // MB

    vmem = pl.BlockSpec(memory_space=pltpu.VMEM)
    hbm = pl.BlockSpec(memory_space=pl.ANY)
    kept = pl.BlockSpec(memory_space=pltpu.HBM)
    assert 2 * dh == LANES
    lines = dh * dh // LANES
    tall = jax.ShapeDtypeStruct((tokens, features), BF16)
    held = pltpu.VMEM((tokens, features), BF16)
    whole = pltpu.VMEM((dh, features), F32)
    part = pltpu.VMEM((dh, half), F32)
    rows = pltpu.VMEM((tokens, features), F32)
    gq, gk, gv, start_rows = pl.pallas_call(
        partial(kernel, dh, width),
        in_specs=[kept] * 4 + [pl.BlockSpec(memory_space=pltpu.SMEM), kept],
        out_specs=[vmem] * 4,
        out_shape=[held, held, held, pltpu.VMEM((lines * heads, LANES), F32)],
        scratch_shapes=[held, held, held, pltpu.SemaphoreType.DMA((3,))] + [
            pltpu.VMEM((features // LANES * dh, LANES), F32),
            pltpu.VMEM((tokens, features), BF16),
            pltpu.VMEM((count * dh, features), F32),
            rows, rows, rows,
            whole, whole,
            part, part, part, part, part, part, part, part, part,
            whole,
            pltpu.SemaphoreType.DMA((lines,)),
            pltpu.SemaphoreType.DMA((2,)),
        ] + [pltpu.SemaphoreType.DMA((chunks,))] * 4
        + [pltpu.SemaphoreType.DMA((half // LANES,))] * 4,
        compiler_params=pltpu.CompilerParams(collective_id=0, has_side_effects=True, vmem_limit_bytes=61 * 2**20 + 2**19),
        name="layer_backward",
    )(upstream[0], queries[0], memory_keys[0], memory_values[0], inner_rate, checkpoints[0, 0])
    gq, gk, gv, start = pl.pallas_call(
        partial(store_kernel, heads),
        in_specs=[hbm] * 4,
        out_specs=[hbm] * 4,
        out_shape=[tall, tall, tall, jax.ShapeDtypeStruct((heads, dh * dh), F32)],
        scratch_shapes=[pltpu.SemaphoreType.DMA((3,)), pltpu.SemaphoreType.DMA((lines,))],
        compiler_params=pltpu.CompilerParams(vmem_limit_bytes=2**20),
        name="store_results",
    )(gq, gk, gv, start_rows)
    return gq[None], gk[None], gv[None], start[None, None]


def solution(mesh):
    return jax.shard_map(
        per_device,
        mesh=mesh,
        in_specs=(
            P("section", "seq", None),
            P("section", "seq", None),
            P("section", "seq", None),
            P("section", "seq", None),
            P("section", None),
            P("section", "seq", None, None),
        ),
        out_specs=(
            P("section", "seq", None),
            P("section", "seq", None),
            P("section", "seq", None),
            P("section", "seq", None, None),
        ),
        check_vma=False,
    )
```
